128 devices in a mesh: grp: 4 (over y_lo, core), hid: 32 (over z, x, y_hi).
Axes of the slice: x: 4, y: 4 (y_hi: 2, y_lo: 2; y = y_hi * 2 + y_lo), z: 4, core: 2. Of those that a mesh axis runs over, the one named last changes fastest.
Arguments:
- states: bfloat16 [8192, 3072], P(('grp', 'hid')), may hold values from -6 to 6
- attention_gain: float32 [3072], replicated, may hold values from 0.1 to 1.9
- forward_gain: float32 [3072], replicated, may hold values from 0.1 to 1.9
- attention_in: float32 [3072, 9216], P('hid'), may hold values from -0.28867513 to 0.28867513
- attention_out: float32 [3072, 3072], P('hid'), may hold values from -0.109375 to 0.109375
- gate_up: float32 [3072, 16384], P('hid'), may hold values from -0.109375 to 0.109375
- down_weight: float32 [8192, 3072], P('hid'), may hold values from -0.0625 to 0.0625
- block_map: int32 [16], replicated, may hold values from 0 to 15, each once
- prompt_lengths: int32 [32], replicated, may hold values from 1 to 32, 640 in all
Outputs:
- hidden_out: bfloat16 [8192, 3072], P(('grp', 'hid'))
- key_cache: bfloat16 [8192, 3072], P('grp', 'hid')
- value_cache: bfloat16 [8192, 3072], P('grp', 'hid')
The draws below stay inside these ranges and needn't reach their ends.
Inputs may be any that keep to these rules, and one draw needn't show every extreme that they name: block_map is a permutation of the 16 logical blocks. prompt_lengths[p] is the number of used slots of short prompt p.
All inputs are finite; a program needn't handle non-finite values.
Results may differ from the reference program's by a relative error of at most 0.02.
Values may be sent and summed in bfloat16 or wider, within the bound.
A program may use at most 192 MiB of HBM per device.

```python
import math
import jax
import jax.numpy as jnp
import numpy as np
from jax import lax

D = 3072
HEADS = 32
HD = 96
FF = 8192
BLOCK = 512
SHORT_LEN = 32
WINDOW = 4096
SINKS = 4
SHORT_BLOCKS = 2
BLOCKS = 16
TOKENS = 8192
NSHORT = 32
N_HID = 32


def draw_attention_in(key, part):
    normal_key = jax.random.fold_in(jax.random.fold_in(key, 17), 0)
    drawn = jnp.clip(jax.random.normal(normal_key, (D, 3 * D), jnp.float32), -4.0, 4.0) * D ** (-0.5)
    return drawn


def block_scale(key, shape, cuts, low, top_value):
    def one(axis_at, parts):
        draws = jax.random.uniform(jax.random.fold_in(jax.random.fold_in(key, 6), axis_at), (parts,), jnp.float32, low / len(cuts), top_value / len(cuts))
        return jnp.repeat(jnp.exp(draws), shape[axis_at] // parts).reshape((-1,) + (1,) * (len(shape) - axis_at - 1))

    factor_of = one(*cuts[0])
    for cut in cuts[1:]:
        factor_of = factor_of * one(*cut)
    return factor_of


def profile(amount, total, most, lean):
    loads = [(1 << 20) // math.isqrt(grade ** lean) + 1 for grade in range(2, amount + 1)]
    surplus, counts = total - most - (amount - 1), [1] * (amount - 1)
    while surplus > 0:
        movable = [i for i in range(amount - 1) if counts[i] < most]
        whole, left = sum([loads[i] for i in movable]), surplus
        for i in movable:
            more = min(most - counts[i], max(1, left * loads[i] // whole), surplus)
            counts[i] = counts[i] + more
            surplus = surplus - more
    return np.array([most] + counts)


def uneven(rng, number_of, total, limit, skew):
    if number_of == 2:
        one = jax.random.randint(rng, (), max(1, total - limit), min(limit, total - 1) + 1)
        return jnp.stack([one, total - one])
    sizes = jnp.asarray(profile(number_of, total, limit, skew), jnp.int32)
    twos = (number_of - 1) // 2
    giver, receiver = sizes[1:1 + 2 * twos:2], sizes[2:2 + 2 * twos:2]
    slack = jnp.minimum(giver - 1, limit - receiver)
    moved = jax.random.randint(jax.random.fold_in(rng, 1), (twos,), 0, 1 << 20) % (slack + 1)
    sizes = sizes.at[1:1 + 2 * twos:2].set(giver - moved).at[2:2 + 2 * twos:2].set(receiver + moved)
    return sizes[jax.random.permutation(jax.random.fold_in(rng, 2), number_of)]


def noise(key, dims, scale, limit, pieces=(), held_as=jnp.bfloat16):
    array = jax.random.normal(key, dims, jnp.float32) * scale
    if len(pieces) > 0:
        array = block_scale(key, dims, pieces, -0.22, 0.18) * array
    return jnp.clip(array, min=-limit, max=limit).astype(held_as)


def setup_inputs(seed: int = 0) -> dict:
    key_of = jax.random.split(jax.random.key(seed), 10)
    states = noise(key_of[0], (TOKENS, D), 1.0, 6.0, ((0, 128),))
    attention_gain = jnp.clip(1.0 + 0.18 * jax.random.normal(key_of[1], (D,), jnp.float32), 0.1, 1.9)
    forward_gain = jnp.clip(1.0 + 0.18 * jax.random.normal(key_of[2], (D,), jnp.float32), 0.1, 1.9)
    attention_in = draw_attention_in(jax.random.fold_in(key_of[9], 71), 0)
    attention_out = noise(key_of[4], (D, D), D ** -0.5, 0.109375, ((0, 32),), jnp.float32)
    gate_up = noise(key_of[5], (D, 2 * FF), D ** -0.5, 0.109375, ((0, 32),), jnp.float32)
    down_weight = noise(key_of[6], (FF, D), FF ** -0.5, 0.0625, ((0, 32),), jnp.float32)
    block_map = jax.random.permutation(key_of[7], BLOCKS).astype(jnp.int32)
    prompt_lengths = uneven(key_of[8], NSHORT, NSHORT * SHORT_LEN * 5 // 8, SHORT_LEN, 1).astype(jnp.int32)
    return dict(states=states, attention_gain=attention_gain, forward_gain=forward_gain, attention_in=attention_in, attention_out=attention_out, gate_up=gate_up, down_weight=down_weight, block_map=block_map, prompt_lengths=prompt_lengths)


EPSILON = 1e-05
ROPE_BASE = 10000.0
MASK_FLOOR = -1e+30

def rms_norm(values, gain):
    widened = values.astype(jnp.float32)
    scaling = lax.rsqrt(lax.optimization_barrier(jnp.mean(widened * widened, axis=-1, keepdims=True)) + EPSILON)
    return (widened * scaling * gain).astype(jnp.bfloat16)

def rotate(values, positions, head_count, head_size):
    half_size = head_size // 2
    inverse = 1.0 / ROPE_BASE ** (jnp.arange(0, head_size, 2).astype(jnp.float32) / head_size)
    angles = positions.astype(jnp.float32)[:, None] * inverse[None, :]
    cosine = jnp.cos(angles)[:, None, :]
    sine_wave = jnp.sin(angles)[:, None, :]
    shaped = values.reshape(values.shape[0], head_count, head_size)
    first_half = shaped[..., :half_size]
    second_half = shaped[..., half_size:]
    turned = jnp.concatenate([first_half * cosine - second_half * sine_wave, second_half * cosine + first_half * sine_wave], axis=-1)
    return turned.reshape(values.shape[0], head_count * head_size)

def block_layout(logical, prompt_lengths, long_blocks):
    offset = jnp.arange(BLOCK, dtype=jnp.int32)
    short_pos = offset % SHORT_LEN
    is_long = logical < long_blocks
    positions = jnp.where(is_long, logical * BLOCK + offset, short_pos)
    prompt = (logical - long_blocks) * (BLOCK // SHORT_LEN) + offset // SHORT_LEN
    matches = prompt[:, None] == jnp.arange(prompt_lengths.shape[0], dtype=jnp.int32)[None, :]
    length = lax.optimization_barrier(jnp.sum(jnp.where(matches, prompt_lengths[None, :], 0), axis=1))
    live_keys = jnp.logical_or(is_long, short_pos < length)
    return (positions, live_keys)

def inverse_map(block_map):
    count_all = block_map.shape[0]
    numbers = jnp.arange(count_all, dtype=jnp.int32)
    matches = block_map[None, :] == numbers[:, None]
    return lax.optimization_barrier(jnp.sum(jnp.where(matches, numbers[None, :], 0), axis=1)).astype(jnp.int32)

def attend(queries, key_rows, value_rows, allowed, head_count):
    query_count = queries.shape[0]
    query_heads = queries.reshape(query_count, head_count, HD).astype(jnp.float32)
    key_heads = key_rows.reshape(key_rows.shape[0], head_count, HD).astype(jnp.float32)
    value_heads = value_rows.reshape(value_rows.shape[0], head_count, HD).astype(jnp.float32)
    scores = jnp.einsum('qhd,khd->hqk', query_heads, key_heads) * HD ** (-0.5)
    scores = jnp.where(allowed[None, :, :], scores, MASK_FLOOR)
    row_peak = lax.optimization_barrier(jnp.max(scores, axis=-1, keepdims=True))
    weights = jnp.exp(scores - row_peak)
    weights = (weights / lax.optimization_barrier(jnp.sum(weights, axis=-1, keepdims=True))).astype(jnp.bfloat16)
    mixed_heads = jnp.einsum('hqk,khd->qhd', weights.astype(jnp.float32), value_heads)
    return mixed_heads.reshape(query_count, head_count * HD).astype(jnp.bfloat16)

def attend_slot(logical, slot_index, queries, key_all, value_all, slot_of, prompt_lengths, long_blocks, head_count):
    width = key_all.shape[1]
    block_count = key_all.shape[0] // BLOCK
    key_blocks = key_all.reshape(block_count, BLOCK, width)
    value_blocks = value_all.reshape(block_count, BLOCK, width)
    offset = jnp.arange(BLOCK, dtype=jnp.int32)
    span = WINDOW // BLOCK

    def long_branch():
        entries = logical - span + jnp.arange(span + 1, dtype=jnp.int32)
        present = jnp.concatenate([entries >= 0, jnp.ones((1,), jnp.bool_)])
        chosen = jnp.concatenate([jnp.maximum(entries, 0), jnp.zeros((1,), jnp.int32)])
        slot_list = slot_of[chosen]
        picked_keys = key_blocks[slot_list].reshape((span + 2) * BLOCK, width)
        picked_values = value_blocks[slot_list].reshape((span + 2) * BLOCK, width)
        key_pos = (chosen[:, None] * BLOCK + offset[None, :]).reshape(-1)
        is_sink = jnp.repeat(jnp.arange(span + 2) == span + 1, BLOCK, total_repeat_length=(span + 2) * BLOCK)
        present_flat = jnp.repeat(present, BLOCK, total_repeat_length=(span + 2) * BLOCK)
        query_pos = logical * BLOCK + offset
        in_window = (key_pos[None, :] <= query_pos[:, None]) & (key_pos[None, :] > query_pos[:, None] - WINDOW) & present_flat[None, :]
        as_sink = (key_pos[None, :] < SINKS) & (key_pos[None, :] <= query_pos[:, None] - WINDOW)
        allowed = jnp.where(is_sink[None, :], as_sink, in_window)
        return attend(queries, picked_keys, picked_values, allowed, head_count)

    def short_branch():
        positions, live_keys = block_layout(logical, prompt_lengths, long_blocks)
        own_keys = key_blocks[slot_index]
        own_values = value_blocks[slot_index]
        segment = offset // SHORT_LEN
        allowed = (segment[:, None] == segment[None, :]) & (positions[None, :] <= positions[:, None]) & live_keys[None, :]
        return attend(queries, own_keys, own_values, allowed, head_count)
    return lax.cond(logical < long_blocks, long_branch, short_branch)

def grouped_sum(left, right, group_count):
    width = left.shape[1] // group_count

    def add_group(running, group_index):
        partial_term = jnp.dot(lax.dynamic_slice_in_dim(left, group_index * width, width, 1), lax.dynamic_slice_in_dim(right, group_index * width, width, 0), preferred_element_type=jnp.float32)
        narrow = lax.optimization_barrier(partial_term.astype(jnp.bfloat16))
        return (running + narrow.astype(jnp.float32), None)
    start_sum = jnp.zeros((left.shape[0], right.shape[1]), jnp.float32)
    result, _ = lax.scan(add_group, start_sum, jnp.arange(group_count, dtype=jnp.int32))
    return result

def reference(states, attention_gain, forward_gain, attention_in, attention_out, gate_up, down_weight, block_map, prompt_lengths):
    token_count = states.shape[0]
    block_count = token_count // BLOCK
    long_blocks = block_count - SHORT_BLOCKS
    normed = rms_norm(states, attention_gain)
    joined = jnp.dot(normed, attention_in.astype(jnp.bfloat16), preferred_element_type=jnp.float32)
    positions, _ = jax.vmap(lambda logical: block_layout(logical, prompt_lengths, long_blocks))(block_map)
    position_flat = positions.reshape(-1)
    queries = rotate(joined[:, :D], position_flat, HEADS, HD).astype(jnp.bfloat16)
    key_cache = rotate(joined[:, D:2 * D], position_flat, HEADS, HD).astype(jnp.bfloat16)
    value_cache = joined[:, 2 * D:].astype(jnp.bfloat16)
    slot_of = inverse_map(block_map)

    def one_block(slot_index):
        logical = block_map[slot_index]
        query_block = lax.dynamic_slice_in_dim(queries, slot_index * BLOCK, BLOCK, 0)
        return attend_slot(logical, slot_index, query_block, key_cache, value_cache, slot_of, prompt_lengths, long_blocks, HEADS)
    attended = lax.map(one_block, jnp.arange(block_count, dtype=jnp.int32)).reshape(token_count, D)
    mixed_sum = grouped_sum(attended, attention_out.astype(jnp.bfloat16), N_HID)
    residual = states.astype(jnp.float32) + mixed_sum
    normed_two = rms_norm(residual, forward_gain)
    lifted = jnp.dot(normed_two, gate_up.astype(jnp.bfloat16), preferred_element_type=jnp.float32)
    activated = (jax.nn.silu(lifted[:, :FF]) * lifted[:, FF:]).astype(jnp.bfloat16)
    forward_sum = grouped_sum(activated, down_weight.astype(jnp.bfloat16), N_HID)
    hidden_out = (residual + forward_sum).astype(jnp.bfloat16)
    return (hidden_out, key_cache, value_cache)
```

```python
import functools

import jax
import jax.numpy as jnp
import numpy as np
from jax import lax
from jax.experimental import pallas as pl
from jax.experimental.pallas import tpu as pltpu
from jax.sharding import Mesh, PartitionSpec as P

HD = 96
BLOCK = 512
SHORT_LEN = 32
WINDOW = 4096
SINKS = 4
SHORT_BLOCKS = 2
EPSILON = 1e-05
ROPE_BASE = 10000.0
MASK_FLOOR = -1e30
LOG2E = 1.4426950408889634

ROWS = 64
PLANE = ("core", "z", "x")


def rms_norm(values, gain):
    widened = values.astype(jnp.float32)
    scaling = lax.rsqrt(jnp.mean(widened * widened, axis=-1, keepdims=True) + EPSILON)
    return (widened * scaling * gain).astype(jnp.bfloat16)


def inverse_map(block_map):
    numbers = jnp.arange(block_map.shape[0], dtype=jnp.int32)
    matches = block_map[None, :] == numbers[:, None]
    return jnp.sum(jnp.where(matches, numbers[None, :], 0), axis=1)


def attention_kernel(
    own_map, slot_of, half_ref, q_ref, k_ref, v_ref, live_ref, o_ref, m_ref, l_ref, acc_ref
):
    step = pl.program_id(0)
    logical = own_map[step]
    own_half = half_ref[0]
    own_lo = half_ref[1]
    scale = HD ** (-0.5) * LOG2E
    rows = q_ref.shape[1]
    q = q_ref[0]

    row_at = lax.broadcasted_iota(jnp.int32, (rows, 2 * rows), 0)
    col_at = lax.broadcasted_iota(jnp.int32, (rows, 2 * rows), 1)
    row_off = (row_at // ROWS) * (2 * ROWS) + own_half * ROWS + row_at % ROWS
    col_in = col_at % rows
    col_off = (col_in // ROWS) * (2 * ROWS) + (col_at // rows) * ROWS + col_in % ROWS

    def pair(slot):
        low = slot // 8
        inner = slot % 8
        keys = jnp.concatenate([k_ref[low * 16 + inner], k_ref[low * 16 + 8 + inner]], axis=0)
        values = jnp.concatenate([v_ref[low * 16 + inner], v_ref[low * 16 + 8 + inner]], axis=0)
        return keys, values

    def scores_of(keys):
        return (
            lax.dot_general(
                q, keys, (((1,), (1,)), ((), ())), preferred_element_type=jnp.float32
            )
            * scale
        )

    def first(scores, values):
        peak = jnp.max(scores, axis=1, keepdims=True)
        weights = jnp.exp2(scores - peak)
        m_ref[...] = peak
        l_ref[...] = jnp.sum(weights, axis=1, keepdims=True)
        acc_ref[...] = jnp.dot(
            weights.astype(jnp.bfloat16), values, preferred_element_type=jnp.float32
        )

    def more(scores, values):
        old = m_ref[...]
        peak = jnp.maximum(old, jnp.max(scores, axis=1, keepdims=True))
        fade = jnp.exp2(old - peak)
        weights = jnp.exp2(scores - peak)
        m_ref[...] = peak
        l_ref[...] = l_ref[...] * fade + jnp.sum(weights, axis=1, keepdims=True)
        acc_ref[...] = acc_ref[...] * fade + jnp.dot(
            weights.astype(jnp.bfloat16), values, preferred_element_type=jnp.float32
        )

    is_long = logical < slot_of.shape[0] - SHORT_BLOCKS
    own_slot = own_lo * 8 + step

    @pl.when(jnp.logical_not(is_long))
    def _():
        keys, values = pair(own_slot)
        allowed = (row_off // SHORT_LEN == col_off // SHORT_LEN) & (col_off <= row_off)
        allowed = allowed & (live_ref[0] > 0.0)
        first(jnp.where(allowed, scores_of(keys), MASK_FLOOR), values)

    @pl.when(is_long)
    def _():
        keys, values = pair(own_slot)
        first(jnp.where(col_off <= row_off, scores_of(keys), MASK_FLOOR), values)
        span = WINDOW // BLOCK
        oldest = jnp.maximum(logical - span + 1, 0)

        def whole(index, carry):
            keys, values = pair(slot_of[index])
            more(scores_of(keys), values)
            return carry

        lax.fori_loop(oldest, logical, whole, 0)

        @pl.when(logical >= span)
        def _():
            edge = logical - span
            keys, values = pair(slot_of[edge])
            allowed = (col_off > row_off) | (edge * BLOCK + col_off < SINKS)
            more(jnp.where(allowed, scores_of(keys), MASK_FLOOR), values)

        @pl.when(logical > span)
        def _():
            slot = slot_of[0]
            at = (slot // 8) * 16 + slot % 8
            keys = k_ref[at, 0:128]
            values = v_ref[at, 0:128]
            allowed = lax.broadcasted_iota(jnp.int32, (rows, 128), 1) < SINKS
            more(jnp.where(allowed, scores_of(keys), MASK_FLOOR), values)

    o_ref[0] = (acc_ref[...] / l_ref[...]).astype(jnp.bfloat16)


def attention(q, k_all, v_all, own_map, slot_of, places, live):
    slots, rows, _ = q.shape
    return pl.pallas_call(
        attention_kernel,
        grid_spec=pltpu.PrefetchScalarGridSpec(
            num_scalar_prefetch=3,
            grid=(slots,),
            in_specs=[
                pl.BlockSpec((1, rows, HD), lambda i, *_: (i, 0, 0)),
                pl.BlockSpec(k_all.shape, lambda i, *_: (0, 0, 0)),
                pl.BlockSpec(v_all.shape, lambda i, *_: (0, 0, 0)),
                pl.BlockSpec((1, 1, 2 * rows), lambda i, *_: (i, 0, 0)),
            ],
            out_specs=pl.BlockSpec((1, rows, HD), lambda i, *_: (i, 0, 0)),
            scratch_shapes=[
                pltpu.VMEM((rows, 1), jnp.float32),
                pltpu.VMEM((rows, 1), jnp.float32),
                pltpu.VMEM((rows, HD), jnp.float32),
            ],
        ),
        out_shape=jax.ShapeDtypeStruct(q.shape, jnp.bfloat16),
        cost_estimate=pl.CostEstimate(
            flops=8_000_000_000, bytes_accessed=8_000_000, transcendentals=8_000_000
        ),
        name="attention",
    )(own_map, slot_of, places, q, k_all, v_all, live)


def rope_tables(positions):
    inverse = 1.0 / ROPE_BASE ** (jnp.arange(0, HD, 2).astype(jnp.float32) / HD)
    angles = positions.astype(jnp.float32)[:, None] * inverse[None, :]
    return jnp.cos(angles), jnp.sin(angles)


def rotate(values, cosine, sine):
    half = HD // 2
    one, two = values[:, :half], values[:, half:]
    return jnp.concatenate(
        [one * cosine - two * sine, two * cosine + one * sine], axis=-1
    ).astype(jnp.bfloat16)


def body(
    states,
    attention_gain,
    forward_gain,
    attention_in,
    attention_out,
    gate_up,
    down_weight,
    block_map,
    prompt_lengths,
):
    width = states.shape[1]
    units = down_weight.shape[0]
    core = lax.axis_index("core")
    y_hi = lax.axis_index("y_hi")
    y_lo = lax.axis_index("y_lo")
    blocks = block_map.shape[0]
    long_blocks = blocks - SHORT_BLOCKS
    rows = 32 * ROWS

    flip = [
        (((a * 2 + c) * 2 + b), (((1 - a) * 2 + c) * 2 + (1 - b)))
        for a in range(2)
        for c in range(2)
        for b in range(2)
    ]
    swap = [
        (((a * 2 + c) * 2 + b), (((1 - a) * 2 + (1 - c)) * 2 + (1 - b)))
        for a in range(2)
        for c in range(2)
        for b in range(2)
        if b != c
    ]

    qkv = attention_in.astype(jnp.bfloat16).reshape(HD, 3, 16, 2, HD)
    gu = gate_up.astype(jnp.bfloat16).reshape(HD, 2, 16, 2, units)

    def spread(full):
        mine = lax.dynamic_index_in_dim(full, core, 3, keepdims=False)
        other = lax.ppermute(mine, ("y_lo", "core", "y_hi"), flip)
        zero = jnp.where(y_hi == 0, mine, other)
        one = jnp.where(y_hi == 0, other, mine)
        both = jnp.stack([zero, one], axis=0)
        both = jnp.transpose(both, (3, 0, 1, 2, 4))
        got = lax.all_to_all(both, ("z", "x"), split_axis=0, concat_axis=0, tiled=True)
        return got.reshape(width, -1)

    def own(shard):
        narrow = shard.astype(jnp.bfloat16)
        other = lax.ppermute(narrow, ("y_lo", "core", "y_hi"), swap)
        return jnp.where(y_hi == core, narrow, other)

    w_qkv = spread(qkv)
    w_gu = spread(gu)
    w_out = own(attention_out)
    w_down = own(down_weight)

    normed = lax.all_gather(rms_norm(states, attention_gain), PLANE, axis=0, tiled=True)
    joined = jnp.dot(normed, w_qkv, preferred_element_type=jnp.float32)

    own_map = lax.dynamic_slice_in_dim(block_map, y_lo * 8, 8)
    at = jnp.arange(256, dtype=jnp.int32)
    at = (at // ROWS) * (2 * ROWS) + at % ROWS
    offset = at + y_hi * ROWS
    positions = jnp.where(
        own_map[:, None] < long_blocks, own_map[:, None] * BLOCK + offset[None], offset % SHORT_LEN
    ).reshape(-1)
    cosine, sine = rope_tables(positions)
    q = rotate(joined[:, :HD], cosine, sine)
    k = rotate(joined[:, HD : 2 * HD], cosine, sine)
    v = joined[:, 2 * HD :].astype(jnp.bfloat16)
    kv = jnp.stack([k, v])
    kv_all = lax.all_gather(kv, ("y_lo", "y_hi"), axis=1)
    kv_all = kv_all.reshape(2, 32, 256, HD)

    offsets = jnp.concatenate([at, at + ROWS])
    prompt = (own_map - long_blocks)[:, None] * (BLOCK // SHORT_LEN) + offsets[None] // SHORT_LEN
    matches = prompt[:, :, None] == jnp.arange(prompt_lengths.shape[0], dtype=jnp.int32)
    length = jnp.sum(jnp.where(matches, prompt_lengths, 0), axis=2)
    live = (offsets[None] % SHORT_LEN < length).astype(jnp.float32)[:, None, :]

    places = jnp.stack([y_hi, y_lo]).astype(jnp.int32)
    attended = attention(
        q.reshape(8, 256, HD), kv_all[0], kv_all[1], own_map, inverse_map(block_map), places, live
    ).reshape(rows, HD)

    group = lax.dynamic_index_in_dim(kv_all.reshape(2, 2, 2, 2, 4, 4, ROWS, HD), y_lo, 1, False)

    def cache_rows(target):
        picked = lax.dynamic_index_in_dim(group, target, 2, False)
        return jnp.transpose(picked, (0, 2, 3, 1, 4, 5)).reshape(2, rows, HD)

    partner = lax.ppermute(
        cache_rows(1 - core),
        ("core", "y_hi"),
        [(b * 2 + b, (1 - b) * 2 + b) for b in range(2)],
    )
    cache = jnp.where(core == y_hi, cache_rows(core), partner)

    def scatter(left, right):
        partial = jnp.dot(left, right, preferred_element_type=jnp.float32).astype(jnp.bfloat16)
        return lax.psum_scatter(partial, PLANE, scatter_dimension=0, tiled=True).astype(
            jnp.float32
        )

    residual = states.astype(jnp.float32) + scatter(attended, w_out)
    normed_two = lax.all_gather(rms_norm(residual, forward_gain), PLANE, axis=0, tiled=True)
    lifted = jnp.dot(normed_two, w_gu, preferred_element_type=jnp.float32)
    activated = (jax.nn.silu(lifted[:, :units]) * lifted[:, units:]).astype(jnp.bfloat16)
    hidden_out = (residual + scatter(activated, w_down)).astype(jnp.bfloat16)
    return (hidden_out, cache[0], cache[1])


def solution(mesh):
    fine = Mesh(mesh.devices.reshape(2, 2, 4, 4, 2), ("y_lo", "core", "z", "x", "y_hi"))
    hid = ("z", "x", "y_hi")
    grp = ("y_lo", "core")
    in_specs = (
        P(grp + hid, None),
        P(),
        P(),
        P(hid, None),
        P(hid, None),
        P(hid, None),
        P(hid, None),
        P(),
        P(),
    )
    out_specs = (P(grp + hid, None), P(grp, hid), P(grp, hid))
    return jax.shard_map(
        body, mesh=fine, in_specs=in_specs, out_specs=out_specs, check_vma=False
    )
```

```python
import functools

import jax
import jax.numpy as jnp
import numpy as np
from jax import lax
from jax.experimental import pallas as pl
from jax.experimental.pallas import tpu as pltpu
from jax.sharding import Mesh, PartitionSpec as P

HD = 96
BLOCK = 512
SHORT_LEN = 32
WINDOW = 4096
SINKS = 4
SHORT_BLOCKS = 2
EPSILON = 1e-05
ROPE_BASE = 10000.0
MASK_FLOOR = -1e30
LOG2E = 1.4426950408889634

ROWS = 64
PLANE = ("core", "z", "x")


def rms_norm(values, gain):
    widened = values.astype(jnp.float32)
    scaling = lax.rsqrt(jnp.mean(widened * widened, axis=-1, keepdims=True) + EPSILON)
    return (widened * scaling * gain).astype(jnp.bfloat16)


def inverse_map(block_map):
    numbers = jnp.arange(block_map.shape[0], dtype=jnp.int32)
    matches = block_map[None, :] == numbers[:, None]
    return jnp.sum(jnp.where(matches, numbers[None, :], 0), axis=1)


def attention_kernel(
    own_map, slot_of, half_ref, q_ref, k_ref, v_ref, live_ref, o_ref, m_ref, l_ref, acc_ref
):
    step = pl.program_id(0)
    logical = own_map[step]
    own_half = half_ref[0]
    own_lo = half_ref[1]
    scale = HD ** (-0.5) * LOG2E
    rows = q_ref.shape[1]
    q = q_ref[0]

    row_at = lax.broadcasted_iota(jnp.int32, (rows, 2 * rows), 0)
    col_at = lax.broadcasted_iota(jnp.int32, (rows, 2 * rows), 1)
    row_off = (row_at // ROWS) * (2 * ROWS) + own_half * ROWS + row_at % ROWS
    col_in = col_at % rows
    col_off = (col_in // ROWS) * (2 * ROWS) + (col_at // rows) * ROWS + col_in % ROWS

    def pair(slot):
        low = slot // 8
        inner = slot % 8
        keys = jnp.concatenate([k_ref[low * 16 + inner], k_ref[low * 16 + 8 + inner]], axis=0)
        values = jnp.concatenate([v_ref[low * 16 + inner], v_ref[low * 16 + 8 + inner]], axis=0)
        return keys, values

    def scores_of(keys):
        return (
            lax.dot_general(
                q, keys, (((1,), (1,)), ((), ())), preferred_element_type=jnp.float32
            )
            * scale
        )

    def first(scores, values):
        peak = jnp.max(scores, axis=1, keepdims=True)
        weights = jnp.exp2(scores - peak)
        m_ref[...] = peak
        l_ref[...] = jnp.sum(weights, axis=1, keepdims=True)
        acc_ref[...] = jnp.dot(
            weights.astype(jnp.bfloat16), values, preferred_element_type=jnp.float32
        )

    def more(scores, values):
        old = m_ref[...]
        peak = jnp.maximum(old, jnp.max(scores, axis=1, keepdims=True))
        fade = jnp.exp2(old - peak)
        weights = jnp.exp2(scores - peak)
        m_ref[...] = peak
        l_ref[...] = l_ref[...] * fade + jnp.sum(weights, axis=1, keepdims=True)
        acc_ref[...] = acc_ref[...] * fade + jnp.dot(
            weights.astype(jnp.bfloat16), values, preferred_element_type=jnp.float32
        )

    is_long = logical < slot_of.shape[0] - SHORT_BLOCKS
    own_slot = own_lo * 8 + step

    @pl.when(jnp.logical_not(is_long))
    def _():
        keys, values = pair(own_slot)
        allowed = (row_off // SHORT_LEN == col_off // SHORT_LEN) & (col_off <= row_off)
        allowed = allowed & (live_ref[0] > 0.0)
        first(jnp.where(allowed, scores_of(keys), MASK_FLOOR), values)

    @pl.when(is_long)
    def _():
        keys, values = pair(own_slot)
        first(jnp.where(col_off <= row_off, scores_of(keys), MASK_FLOOR), values)
        span = WINDOW // BLOCK
        oldest = jnp.maximum(logical - span + 1, 0)

        def whole(index, carry):
            keys, values = pair(slot_of[index])
            more(scores_of(keys), values)
            return carry

        lax.fori_loop(oldest, logical, whole, 0)

        @pl.when(logical >= span)
        def _():
            edge = logical - span
            keys, values = pair(slot_of[edge])
            allowed = (col_off > row_off) | (edge * BLOCK + col_off < SINKS)
            more(jnp.where(allowed, scores_of(keys), MASK_FLOOR), values)

        @pl.when(logical > span)
        def _():
            slot = slot_of[0]
            at = (slot // 8) * 16 + slot % 8
            keys = k_ref[at, 0:128]
            values = v_ref[at, 0:128]
            allowed = lax.broadcasted_iota(jnp.int32, (rows, 128), 1) < SINKS
            more(jnp.where(allowed, scores_of(keys), MASK_FLOOR), values)

    o_ref[0] = (acc_ref[...] / l_ref[...]).astype(jnp.bfloat16)


def attention(q, k_all, v_all, own_map, slot_of, places, live):
    slots, rows, _ = q.shape
    return pl.pallas_call(
        attention_kernel,
        grid_spec=pltpu.PrefetchScalarGridSpec(
            num_scalar_prefetch=3,
            grid=(slots,),
            in_specs=[
                pl.BlockSpec((1, rows, HD), lambda i, *_: (i, 0, 0)),
                pl.BlockSpec(k_all.shape, lambda i, *_: (0, 0, 0)),
                pl.BlockSpec(v_all.shape, lambda i, *_: (0, 0, 0)),
                pl.BlockSpec((1, 1, 2 * rows), lambda i, *_: (i, 0, 0)),
            ],
            out_specs=pl.BlockSpec((1, rows, HD), lambda i, *_: (i, 0, 0)),
            scratch_shapes=[
                pltpu.VMEM((rows, 1), jnp.float32),
                pltpu.VMEM((rows, 1), jnp.float32),
                pltpu.VMEM((rows, HD), jnp.float32),
            ],
        ),
        out_shape=jax.ShapeDtypeStruct(q.shape, jnp.bfloat16),
        cost_estimate=pl.CostEstimate(
            flops=8_000_000_000, bytes_accessed=8_000_000, transcendentals=8_000_000
        ),
        name="attention",
    )(own_map, slot_of, places, q, k_all, v_all, live)


MESH = pl.DeviceIdType.MESH
HALF = ROWS // 2


def ring(axis):
    me = lax.axis_index(axis)
    return me, lax.rem(me + 1, 4), lax.rem(me + 3, 4), lax.rem(me + 2, 4)


def meet():
    barrier = pltpu.get_barrier_semaphore()
    for axis in ("x", "z"):
        _, right, left, _ = ring(axis)
        for peer in (right, left):
            pl.semaphore_signal(barrier, inc=1, device_id={axis: peer}, device_id_type=MESH)
    pl.semaphore_signal(
        barrier, inc=1, device_id={"core": 1 - lax.axis_index("core")}, device_id_type=MESH
    )
    pl.semaphore_wait(barrier, 5)


def push(src, dst, sems, at, axis, peer):
    send, recv = sems
    return pltpu.make_async_remote_copy(
        src_ref=src,
        dst_ref=dst,
        send_sem=send.at[at],
        recv_sem=recv.at[at],
        device_id={axis: peer},
        device_id_type=MESH,
    )


def scatter_steps(
    make, other, held, near, early, late, early_two, late_two, total, sems, finish
):
    core = lax.axis_index("core")
    rings = (ring("z"), ring("x"))
    axes = ("z", "x")
    copies = []

    def go(copy):
        copy.start()
        copies.append(copy)
        return copy

    def big_at(half, step):
        me, right, left, far = rings[half]
        return (far, right, left, me)[step]

    swaps = {}
    for step in range(4):
        for half in range(2):
            at = half * 4 + step
            make(other.at[half, step], None, half, 1 - core, big_at(half, step))
            swaps[half, step] = go(
                push(
                    other.at[half, step],
                    near.at[half, step],
                    sems[0],
                    at,
                    "core",
                    1 - core,
                )
            )

    first = {}
    second = {}
    for half in range(2):
        _, right, left, _ = rings[half]
        swaps[half, 0].wait_recv()
        make(held.at[half, 0], near.at[half, 0], half, core, big_at(half, 0))
        for side, peer in ((0, right), (1, left)):
            first[half, side] = go(
                push(
                    held.at[half, 0, pl.ds(2 * side, 2)],
                    early.at[half, side],
                    sems[1],
                    half * 2 + side,
                    axes[half],
                    peer,
                )
            )
    for side in range(2):
        for half in range(2):
            _, right, left, _ = rings[half]
            step = 1 + side
            swaps[half, step].wait_recv()
            make(held.at[half, step], near.at[half, step], half, core, big_at(half, step))
            first[half, side].wait_recv()
            part = held.at[half, step, pl.ds(2 * side, 2)]
            part[...] = (
                part[...].astype(jnp.float32) + early[half, side].astype(jnp.float32)
            ).astype(jnp.bfloat16)
            second[half, side] = go(
                push(
                    held.at[half, step],
                    late.at[half, side],
                    sems[2],
                    half * 2 + side,
                    axes[half],
                    (right, left)[side],
                )
            )
    for half in range(2):
        swaps[half, 3].wait_recv()
        make(held.at[half, 3], near.at[half, 3], half, core, big_at(half, 3))

    def small_at(half, step):
        me, right, left, far = rings[1 - half]
        return (far, right, left, me)[step]

    third = {}
    fourth = {}

    def gather_small(half, step):
        at = small_at(half, step)
        total[half, step] = (
            held[half, 3, at].astype(jnp.float32)
            + late[half, 0, at].astype(jnp.float32)
            + late[half, 1, at].astype(jnp.float32)
        ).astype(jnp.bfloat16)

    for half in range(2):
        _, right, left, _ = rings[1 - half]
        for side in range(2):
            second[half, side].wait_recv()
        gather_small(half, 0)
        for side, peer in ((0, right), (1, left)):
            third[half, side] = go(
                push(
                    total.at[half, 0, pl.ds(16 * side, 16)],
                    early_two.at[half, side],
                    sems[3],
                    half * 2 + side,
                    axes[1 - half],
                    peer,
                )
            )
        gather_small(half, 1)
        gather_small(half, 2)
    for side in range(2):
        for half in range(2):
            _, right, left, _ = rings[1 - half]
            third[half, side].wait_recv()
            part = total.at[half, 1 + side, pl.ds(16 * side, 16)]
            part[...] = (
                part[...].astype(jnp.float32) + early_two[half, side].astype(jnp.float32)
            ).astype(jnp.bfloat16)
            fourth[half, side] = go(
                push(
                    total.at[half, 1 + side],
                    late_two.at[half, side],
                    sems[4],
                    half * 2 + side,
                    axes[1 - half],
                    (right, left)[side],
                )
            )
    for half in range(2):
        at = small_at(half, 3)
        for side in range(2):
            fourth[half, side].wait_recv()
        finish(
            half,
            held[half, 3, at].astype(jnp.float32)
            + late[half, 0, at].astype(jnp.float32)
            + late[half, 1, at].astype(jnp.float32)
            + late_two[half, 0].astype(jnp.float32)
            + late_two[half, 1].astype(jnp.float32),
        )
    for copy in copies:
        copy.wait_send()


def scatter_scratch(width):
    return [
        pltpu.VMEM((2, 4, 4, HALF, width), jnp.bfloat16),
        pltpu.VMEM((2, 4, 4, HALF, width), jnp.bfloat16),
        pltpu.VMEM((2, 4, 4, HALF, width), jnp.bfloat16),
        pltpu.VMEM((2, 2, 2, HALF, width), jnp.bfloat16),
        pltpu.VMEM((2, 2, 4, HALF, width), jnp.bfloat16),
        pltpu.VMEM((2, 2, 16, width), jnp.bfloat16),
        pltpu.VMEM((2, 2, HALF, width), jnp.bfloat16),
        pltpu.VMEM((2, 3, HALF, width), jnp.bfloat16),
    ] + [pltpu.SemaphoreType.DMA((n,)) for n in (8, 8, 4, 4, 4, 4, 4, 4, 4, 4)]


def scatter_scope(left_ref, right_ref, scratch, finish):
    width = right_ref.shape[1]
    depth = right_ref.shape[0]
    tile = 512
    other, held, near, early, late, early_two, late_two, total = scratch[:8]
    flat = scratch[8:]
    sems = [(flat[2 * i], flat[2 * i + 1]) for i in range(5)]

    def make(dst, add, half, core, big):
        if half == 0:
            rows = left_ref[core, big, :, 0:HALF, :]
        else:
            rows = left_ref[core, :, big, HALF:ROWS, :]
        rows = rows.reshape(4 * HALF, depth)

        def column(i, carry):
            cols = pl.ds(pl.multiple_of(i * tile, tile), tile)
            value = jnp.dot(rows, right_ref[:, cols], preferred_element_type=jnp.float32)
            value = value.reshape(4, HALF, tile)
            if add is not None:
                value = value + add[:, :, cols].astype(jnp.float32)
            dst[:, :, cols] = value.astype(jnp.bfloat16)
            return carry

        lax.fori_loop(0, width // tile, column, 0)

    scatter_steps(
        make, other, held, near, early, late, early_two, late_two, total, sems, finish
    )


def mix_kernel(left_ref, right_ref, base_ref, gain_ref, res_ref, normed_ref, *scratch):
    meet()

    def finish(half, value):
        rows = pl.ds(half * HALF, HALF)
        value = value + base_ref[rows, :].astype(jnp.float32)
        res_ref[rows, :] = value
        scaling = lax.rsqrt(jnp.mean(value * value, axis=-1, keepdims=True) + EPSILON)
        normed_ref[rows, :] = (value * scaling * gain_ref[...]).astype(jnp.bfloat16)

    scatter_scope(left_ref, right_ref, scratch, finish)


def down_kernel(left_ref, right_ref, base_ref, out_ref, *scratch):
    meet()

    def finish(half, value):
        rows = pl.ds(half * HALF, HALF)
        out_ref[rows, :] = (value + base_ref[rows, :]).astype(jnp.bfloat16)

    scatter_scope(left_ref, right_ref, scratch, finish)


VM = pl.BlockSpec(memory_space=pltpu.VMEM)


def remote_params(number):
    return pltpu.CompilerParams(
        collective_id=number, has_side_effects=True, vmem_limit_bytes=60 * 1024 * 1024
    )


def mix(left, right, base, gain):
    width = right.shape[1]
    return pl.pallas_call(
        mix_kernel,
        in_specs=[VM] * 4,
        out_specs=[VM] * 2,
        out_shape=[
            jax.ShapeDtypeStruct((ROWS, width), jnp.float32),
            jax.ShapeDtypeStruct((ROWS, width), jnp.bfloat16),
        ],
        scratch_shapes=scatter_scratch(width),
        compiler_params=remote_params(1),
        name="mix",
    )(left.reshape(2, 4, 4, ROWS, -1), right, base, gain.reshape(1, width))


def down(left, right, base):
    width = right.shape[1]
    return pl.pallas_call(
        down_kernel,
        in_specs=[VM] * 3,
        out_specs=VM,
        out_shape=jax.ShapeDtypeStruct((ROWS, width), jnp.bfloat16),
        scratch_shapes=scatter_scratch(width),
        compiler_params=remote_params(2),
        name="down",
    )(left.reshape(2, 4, 4, ROWS, -1), right, base)


def gather_steps(x_ref, buf, sems, use):
    core = lax.axis_index("core")
    axes = ("z", "x")
    rings = (ring("z"), ring("x"))
    copies = []

    def go(copy):
        copy.start()
        copies.append(copy)
        return copy

    def spot(half, big, small, c=None):
        return buf.at[half, big, core if c is None else c, small]

    one = {}
    cores = {}
    for half in range(2):
        big = rings[half][0]
        me, right, left, _ = rings[1 - half]
        buf[half, big, core, me] = x_ref[half * HALF : (half + 1) * HALF, :]
        for side, peer in ((0, right), (1, left)):
            one[half, side] = go(
                push(
                    x_ref.at[pl.ds(half * HALF, HALF)],
                    spot(half, big, me),
                    sems[0],
                    half * 2 + side,
                    axes[1 - half],
                    peer,
                )
            )
        cores[half, 0] = go(
            push(
                x_ref.at[pl.ds(half * HALF, HALF)],
                spot(half, big, me),
                sems[1],
                half * 4,
                "core",
                1 - core,
            )
        )
    two = {}
    for half in range(2):
        big = rings[half][0]
        me, right, left, far = rings[1 - half]
        for side, (frm, to) in ((0, (left, right)), (1, (right, left))):
            one[half, side].wait_recv()
            piece = buf.at[half, big, core, frm, pl.ds(16 * side, 16)]
            two[half, side] = go(
                push(piece, piece, sems[2], half * 2 + side, axes[1 - half], to)
            )
            whole = spot(half, big, frm)
            cores[half, 1 + side] = go(
                push(whole, whole, sems[1], half * 4 + 1 + side, "core", 1 - core)
            )
    three = {}
    for half in range(2):
        big, right, left, _ = rings[half]
        far = rings[1 - half][3]
        for side in range(2):
            two[half, side].wait_recv()
        whole = spot(half, big, far)
        chunk = buf.at[half, big, core]
        for side, peer in ((0, right), (1, left)):
            three[half, side] = go(
                push(chunk, chunk, sems[3], half * 2 + side, axes[half], peer)
            )
        cores[half, 3] = go(push(whole, whole, sems[1], half * 4 + 3, "core", 1 - core))
    for half in range(2):
        for i in range(4):
            cores[half, i].wait_recv()
        use(half, rings[half][0])
    four = {}
    fives = {}
    for half in range(2):
        big, right, left, far = rings[half]
        for side, (frm, to) in ((0, (left, right)), (1, (right, left))):
            three[half, side].wait_recv()
            piece = buf.at[half, frm, core, pl.ds(2 * side, 2)]
            four[half, side] = go(push(piece, piece, sems[4], half * 2 + side, axes[half], to))
            chunk = buf.at[half, frm, core]
            fives[half, side] = go(
                push(chunk, chunk, sems[5], half * 4 + side, "core", 1 - core)
            )
    for half in range(2):
        _, right, left, _ = rings[half]
        for side, frm in ((0, left), (1, right)):
            fives[half, side].wait_recv()
            use(half, frm)
    for half in range(2):
        far = rings[half][3]
        for side in range(2):
            four[half, side].wait_recv()
            piece = buf.at[half, far, core, pl.ds(2 * side, 2)]
            fives[half, 2 + side] = go(
                push(piece, piece, sems[5], half * 4 + 2 + side, "core", 1 - core)
            )
    for half in range(2):
        for side in range(2):
            fives[half, 2 + side].wait_recv()
        use(half, rings[half][3])
    for copy in copies:
        copy.wait_send()


def gather_scratch(width):
    return [pltpu.VMEM((2, 4, 2, 4, HALF, width), jnp.bfloat16)] + [
        pltpu.SemaphoreType.DMA((n,)) for n in (4, 4, 8, 8, 4, 4, 4, 4, 4, 4, 8, 8)
    ]


def gather_scope(x_ref, scratch, use):
    buf = scratch[0]
    sems = [(scratch[1 + 2 * i], scratch[2 + 2 * i]) for i in range(6)]
    gather_steps(x_ref, buf, sems, use)


def project_kernel(x_ref, w_ref, out_ref, *scratch):
    meet()
    buf = scratch[0]

    def use(half, big):
        rows = buf[half, big].reshape(8 * HALF, x_ref.shape[1])
        value = jnp.dot(rows, w_ref[...], preferred_element_type=jnp.float32)
        value = value.reshape(2, 4, HALF, w_ref.shape[1])
        if half == 0:
            out_ref[:, big, :, 0:HALF, :] = value
        else:
            out_ref[:, :, big, HALF:ROWS, :] = value

    gather_scope(x_ref, scratch, use)


def lift_kernel(x_ref, w_ref, out_ref, *scratch):
    meet()
    buf = scratch[0]
    units = out_ref.shape[-1]

    def use(half, big):
        rows = buf[half, big].reshape(8 * HALF, x_ref.shape[1])
        value = jnp.dot(rows, w_ref[...], preferred_element_type=jnp.float32)
        gate, up = value[:, :units], value[:, units:]
        value = (gate / (1.0 + jnp.exp(-gate)) * up).astype(jnp.bfloat16)
        value = value.reshape(2, 4, HALF, units)
        if half == 0:
            out_ref[:, big, :, 0:HALF, :] = value
        else:
            out_ref[:, :, big, HALF:ROWS, :] = value

    gather_scope(x_ref, scratch, use)


def project(x, w):
    n = w.shape[1]
    return pl.pallas_call(
        project_kernel,
        in_specs=[VM] * 2,
        out_specs=VM,
        out_shape=jax.ShapeDtypeStruct((2, 4, 4, ROWS, n), jnp.float32),
        scratch_shapes=gather_scratch(x.shape[1]),
        compiler_params=remote_params(3),
        name="project",
    )(x, w).reshape(32 * ROWS, n)


def lift(x, w):
    units = w.shape[1] // 2
    return pl.pallas_call(
        lift_kernel,
        in_specs=[VM] * 2,
        out_specs=VM,
        out_shape=jax.ShapeDtypeStruct((2, 4, 4, ROWS, units), jnp.bfloat16),
        scratch_shapes=gather_scratch(x.shape[1]),
        compiler_params=remote_params(4),
        name="lift",
    )(x, w).reshape(32 * ROWS, units)


def rope_tables(positions):
    inverse = 1.0 / ROPE_BASE ** (jnp.arange(0, HD, 2).astype(jnp.float32) / HD)
    angles = positions.astype(jnp.float32)[:, None] * inverse[None, :]
    return jnp.cos(angles), jnp.sin(angles)


def rotate(values, cosine, sine):
    half = HD // 2
    one, two = values[:, :half], values[:, half:]
    return jnp.concatenate(
        [one * cosine - two * sine, two * cosine + one * sine], axis=-1
    ).astype(jnp.bfloat16)


def body(
    states,
    attention_gain,
    forward_gain,
    attention_in,
    attention_out,
    gate_up,
    down_weight,
    block_map,
    prompt_lengths,
):
    width = states.shape[1]
    units = down_weight.shape[0]
    core = lax.axis_index("core")
    y_hi = lax.axis_index("y_hi")
    y_lo = lax.axis_index("y_lo")
    blocks = block_map.shape[0]
    long_blocks = blocks - SHORT_BLOCKS
    rows = 32 * ROWS

    flip = [
        (((a * 2 + c) * 2 + b), (((1 - a) * 2 + c) * 2 + (1 - b)))
        for a in range(2)
        for c in range(2)
        for b in range(2)
    ]
    swap = [
        (((a * 2 + c) * 2 + b), (((1 - a) * 2 + (1 - c)) * 2 + (1 - b)))
        for a in range(2)
        for c in range(2)
        for b in range(2)
        if b != c
    ]

    qkv = attention_in.astype(jnp.bfloat16).reshape(HD, 3, 16, 2, HD)
    gu = gate_up.astype(jnp.bfloat16).reshape(HD, 2, 16, 2, units)

    def spread(full):
        mine = lax.dynamic_index_in_dim(full, core, 3, keepdims=False)
        other = lax.ppermute(mine, ("y_lo", "core", "y_hi"), flip)
        zero = jnp.where(y_hi == 0, mine, other)
        one = jnp.where(y_hi == 0, other, mine)
        both = jnp.stack([zero, one], axis=0)
        both = jnp.transpose(both, (3, 0, 1, 2, 4))
        got = lax.all_to_all(both, ("z", "x"), split_axis=0, concat_axis=0, tiled=True)
        return got.reshape(width, -1)

    def own(shard):
        narrow = shard.astype(jnp.bfloat16)
        other = lax.ppermute(narrow, ("y_lo", "core", "y_hi"), swap)
        return jnp.where(y_hi == core, narrow, other)

    w_qkv = spread(qkv)
    w_gu = spread(gu)
    w_out = own(attention_out)
    w_down = own(down_weight)

    joined = project(rms_norm(states, attention_gain), w_qkv)

    own_map = lax.dynamic_slice_in_dim(block_map, y_lo * 8, 8)
    at = jnp.arange(256, dtype=jnp.int32)
    at = (at // ROWS) * (2 * ROWS) + at % ROWS
    offset = at + y_hi * ROWS
    positions = jnp.where(
        own_map[:, None] < long_blocks, own_map[:, None] * BLOCK + offset[None], offset % SHORT_LEN
    ).reshape(-1)
    cosine, sine = rope_tables(positions)
    q = rotate(joined[:, :HD], cosine, sine)
    k = rotate(joined[:, HD : 2 * HD], cosine, sine)
    v = joined[:, 2 * HD :].astype(jnp.bfloat16)
    kv = jnp.stack([k, v])
    kv_all = lax.all_gather(kv, ("y_lo", "y_hi"), axis=1)
    kv_all = kv_all.reshape(2, 32, 256, HD)

    offsets = jnp.concatenate([at, at + ROWS])
    prompt = (own_map - long_blocks)[:, None] * (BLOCK // SHORT_LEN) + offsets[None] // SHORT_LEN
    matches = prompt[:, :, None] == jnp.arange(prompt_lengths.shape[0], dtype=jnp.int32)
    length = jnp.sum(jnp.where(matches, prompt_lengths, 0), axis=2)
    live = (offsets[None] % SHORT_LEN < length).astype(jnp.float32)[:, None, :]

    places = jnp.stack([y_hi, y_lo]).astype(jnp.int32)
    attended = attention(
        q.reshape(8, 256, HD), kv_all[0], kv_all[1], own_map, inverse_map(block_map), places, live
    ).reshape(rows, HD)

    group = lax.dynamic_index_in_dim(kv_all.reshape(2, 2, 2, 2, 4, 4, ROWS, HD), y_lo, 1, False)

    def cache_rows(target):
        picked = lax.dynamic_index_in_dim(group, target, 2, False)
        return jnp.transpose(picked, (0, 2, 3, 1, 4, 5)).reshape(2, rows, HD)

    partner = lax.ppermute(
        cache_rows(1 - core),
        ("core", "y_hi"),
        [(b * 2 + b, (1 - b) * 2 + b) for b in range(2)],
    )
    cache = jnp.where(core == y_hi, cache_rows(core), partner)

    residual, normed_two = mix(attended, w_out, states, forward_gain)
    activated = lift(normed_two, w_gu)
    hidden_out = down(activated, w_down, residual)
    return (hidden_out, cache[0], cache[1])


def solution(mesh):
    fine = Mesh(mesh.devices.reshape(2, 2, 4, 4, 2), ("y_lo", "core", "z", "x", "y_hi"))
    hid = ("z", "x", "y_hi")
    grp = ("y_lo", "core")
    in_specs = (
        P(grp + hid, None),
        P(),
        P(),
        P(hid, None),
        P(hid, None),
        P(hid, None),
        P(hid, None),
        P(),
        P(),
    )
    out_specs = (P(grp + hid, None), P(grp, hid), P(grp, hid))
    return jax.shard_map(
        body, mesh=fine, in_specs=in_specs, out_specs=out_specs, check_vma=False
    )
```

```python
import functools

import jax
import jax.numpy as jnp
import numpy as np
from jax import lax
from jax.experimental import pallas as pl
from jax.experimental.pallas import tpu as pltpu
from jax.sharding import Mesh, PartitionSpec as P

HD = 96
BLOCK = 512
SHORT_LEN = 32
WINDOW = 4096
SINKS = 4
SHORT_BLOCKS = 2
EPSILON = 1e-05
ROPE_BASE = 10000.0
MASK_FLOOR = -1e30
LOG2E = 1.4426950408889634

ROWS = 64
PLANE = ("core", "z", "x")


def rms_norm(values, gain):
    widened = values.astype(jnp.float32)
    scaling = lax.rsqrt(jnp.mean(widened * widened, axis=-1, keepdims=True) + EPSILON)
    return (widened * scaling * gain).astype(jnp.bfloat16)


def inverse_map(block_map):
    numbers = jnp.arange(block_map.shape[0], dtype=jnp.int32)
    matches = block_map[None, :] == numbers[:, None]
    return jnp.sum(jnp.where(matches, numbers[None, :], 0), axis=1)


def attention_kernel(
    own_map, slot_of, half_ref, q_ref, kv_ref, live_ref, o_ref, m_ref, l_ref, acc_ref
):
    step = pl.program_id(0)
    logical = own_map[step]
    own_half = half_ref[0]
    own_lo = half_ref[1]
    scale = HD ** (-0.5) * LOG2E
    rows = q_ref.shape[1]
    q = q_ref[0]

    row_at = lax.broadcasted_iota(jnp.int32, (rows, 2 * rows), 0)
    col_at = lax.broadcasted_iota(jnp.int32, (rows, 2 * rows), 1)
    row_off = (row_at // ROWS) * (2 * ROWS) + own_half * ROWS + row_at % ROWS
    col_in = col_at % rows
    col_off = (col_in // ROWS) * (2 * ROWS) + (col_at // rows) * ROWS + col_in % ROWS

    def pair(slot):
        low = slot // 8
        inner = slot % 8
        keys = jnp.concatenate([kv_ref[low, 0, inner], kv_ref[low + 2, 0, inner]], axis=0)
        values = jnp.concatenate([kv_ref[low, 1, inner], kv_ref[low + 2, 1, inner]], axis=0)
        return keys, values

    def scores_of(keys):
        return (
            lax.dot_general(
                q, keys, (((1,), (1,)), ((), ())), preferred_element_type=jnp.float32
            )
            * scale
        )

    def first(scores, values):
        peak = jnp.max(scores, axis=1, keepdims=True)
        weights = jnp.exp2(scores - peak)
        m_ref[...] = peak
        l_ref[...] = jnp.sum(weights, axis=1, keepdims=True)
        acc_ref[...] = jnp.dot(
            weights.astype(jnp.bfloat16), values, preferred_element_type=jnp.float32
        )

    def more(scores, values):
        old = m_ref[...]
        peak = jnp.maximum(old, jnp.max(scores, axis=1, keepdims=True))
        fade = jnp.exp2(old - peak)
        weights = jnp.exp2(scores - peak)
        m_ref[...] = peak
        l_ref[...] = l_ref[...] * fade + jnp.sum(weights, axis=1, keepdims=True)
        acc_ref[...] = acc_ref[...] * fade + jnp.dot(
            weights.astype(jnp.bfloat16), values, preferred_element_type=jnp.float32
        )

    is_long = logical < slot_of.shape[0] - SHORT_BLOCKS
    own_slot = own_lo * 8 + step

    @pl.when(jnp.logical_not(is_long))
    def _():
        keys, values = pair(own_slot)
        allowed = (row_off // SHORT_LEN == col_off // SHORT_LEN) & (col_off <= row_off)
        allowed = allowed & (live_ref[0] > 0.0)
        first(jnp.where(allowed, scores_of(keys), MASK_FLOOR), values)

    @pl.when(is_long)
    def _():
        keys, values = pair(own_slot)
        first(jnp.where(col_off <= row_off, scores_of(keys), MASK_FLOOR), values)
        span = WINDOW // BLOCK
        oldest = jnp.maximum(logical - span + 1, 0)

        def whole(index, carry):
            keys, values = pair(slot_of[index])
            more(scores_of(keys), values)
            return carry

        lax.fori_loop(oldest, logical, whole, 0)

        @pl.when(logical >= span)
        def _():
            edge = logical - span
            keys, values = pair(slot_of[edge])
            allowed = (col_off > row_off) | (edge * BLOCK + col_off < SINKS)
            more(jnp.where(allowed, scores_of(keys), MASK_FLOOR), values)

        @pl.when(logical > span)
        def _():
            slot = slot_of[0]
            keys = kv_ref[slot // 8, 0, slot % 8, 0:128]
            values = kv_ref[slot // 8, 1, slot % 8, 0:128]
            allowed = lax.broadcasted_iota(jnp.int32, (rows, 128), 1) < SINKS
            more(jnp.where(allowed, scores_of(keys), MASK_FLOOR), values)

    o_ref[0] = (acc_ref[...] / l_ref[...]).astype(jnp.bfloat16)


def attention(q, kv, own_map, slot_of, places, live):
    slots, rows, _ = q.shape
    return pl.pallas_call(
        attention_kernel,
        grid_spec=pltpu.PrefetchScalarGridSpec(
            num_scalar_prefetch=3,
            grid=(slots,),
            in_specs=[
                pl.BlockSpec((1, rows, HD), lambda i, *_: (i, 0, 0)),
                pl.BlockSpec(kv.shape, lambda i, *_: (0, 0, 0, 0, 0)),
                pl.BlockSpec((1, 1, 2 * rows), lambda i, *_: (i, 0, 0)),
            ],
            out_specs=pl.BlockSpec((1, rows, HD), lambda i, *_: (i, 0, 0)),
            scratch_shapes=[
                pltpu.VMEM((rows, 1), jnp.float32),
                pltpu.VMEM((rows, 1), jnp.float32),
                pltpu.VMEM((rows, HD), jnp.float32),
            ],
        ),
        out_shape=jax.ShapeDtypeStruct(q.shape, jnp.bfloat16),
        cost_estimate=pl.CostEstimate(
            flops=8_000_000_000, bytes_accessed=8_000_000, transcendentals=8_000_000
        ),
        name="attention",
    )(own_map, slot_of, places, q, kv, live)


MESH = pl.DeviceIdType.MESH
HALF = ROWS // 2


def ring(axis):
    me = lax.axis_index(axis)
    return me, lax.rem(me + 1, 4), lax.rem(me + 3, 4), lax.rem(me + 2, 4)


def ring_y():
    me = lax.axis_index("y_hi") * 2 + lax.axis_index("y_lo")
    return me, lax.rem(me + 1, 4), lax.rem(me + 3, 4), lax.rem(me + 2, 4)


def at_y(y):
    return {"y_hi": lax.div(y, 2), "y_lo": lax.rem(y, 2)}


def at_offset(offset):
    z, x = lax.axis_index("z"), lax.axis_index("x")
    return {"z": lax.rem(z + offset // 4, 4), "x": lax.rem(x + offset % 4, 4)}


def meet(whole=False):
    barrier = pltpu.get_barrier_semaphore()
    peers = [{"core": 1 - lax.axis_index("core")}]
    if whole:
        peers += [at_offset(offset) for offset in range(1, 16)]
        peers += [at_y(y) for y in ring_y()[1:3]]
    else:
        for axis in ("x", "z"):
            peers += [{axis: peer} for peer in ring(axis)[1:3]]
    for peer in peers:
        pl.semaphore_signal(barrier, inc=1, device_id=peer, device_id_type=MESH)
    pl.semaphore_wait(barrier, len(peers))


def push(src, dst, sems, at, axis, peer):
    send, recv = sems
    place = peer if axis is None else {axis: peer}
    return pltpu.make_async_remote_copy(
        src_ref=src,
        dst_ref=dst,
        send_sem=send.at[at],
        recv_sem=recv.at[at],
        device_id=place,
        device_id_type=MESH,
    )


class Spread:
    def __init__(self, parts, full, sems):
        self.parts, self.full, self.sems = parts, full, sems
        self.copies = []

    def go(self, copy):
        copy.start()
        self.copies.append(copy)
        return copy

    def send(self):
        me = lax.axis_index("z") * 4 + lax.axis_index("x")
        y = ring_y()[0]
        self.full[me, y] = self.parts[me]
        self.one = []
        for offset in range(1, 16):
            place = at_offset(offset)
            self.one.append(
                self.go(
                    push(
                        self.parts.at[place["z"] * 4 + place["x"]],
                        self.full.at[me, y],
                        self.sems[0],
                        offset,
                        None,
                        place,
                    )
                )
            )

    def along(self):
        for copy in self.one:
            copy.wait_recv()
        me, right, left, _ = ring_y()
        piece = self.full.at[:, me]
        self.two = [
            self.go(push(piece, piece, self.sems[1], side, None, at_y(peer)))
            for side, peer in ((0, right), (1, left))
        ]

    def relay(self):
        _, right, left, _ = ring_y()
        self.three = []
        for side, (frm, to) in ((0, (left, right)), (1, (right, left))):
            self.two[side].wait_recv()
            piece = self.full.at[pl.ds(8 * side, 8), frm]
            self.three.append(
                self.go(push(piece, piece, self.sems[2], side, None, at_y(to)))
            )

    def arrive(self):
        for copy in self.three:
            copy.wait_recv()

    def done(self):
        for copy in self.copies:
            copy.wait_send()


def spread_sems():
    return [pltpu.SemaphoreType.DMA((n,)) for n in (16, 16, 2, 2, 2, 2)]


def paired(flat):
    return [(flat[2 * i], flat[2 * i + 1]) for i in range(len(flat) // 2)]


def scatter_steps(
    make, other, held, near, early, late, early_two, late_two, total, sems, finish, hook
):
    core = lax.axis_index("core")
    rings = (ring("z"), ring("x"))
    axes = ("z", "x")
    copies = []

    def go(copy):
        copy.start()
        copies.append(copy)
        return copy

    def big_at(half, step):
        me, right, left, far = rings[half]
        return (far, right, left, me)[step]

    swaps = {}
    for step in range(4):
        for half in range(2):
            at = half * 4 + step
            make(other.at[half, step], None, half, 1 - core, big_at(half, step))
            swaps[half, step] = go(
                push(
                    other.at[half, step],
                    near.at[half, step],
                    sems[0],
                    at,
                    "core",
                    1 - core,
                )
            )

    hook(0)
    first = {}
    second = {}
    for half in range(2):
        _, right, left, _ = rings[half]
        swaps[half, 0].wait_recv()
        make(held.at[half, 0], near.at[half, 0], half, core, big_at(half, 0))
        for side, peer in ((0, right), (1, left)):
            first[half, side] = go(
                push(
                    held.at[half, 0, pl.ds(2 * side, 2)],
                    early.at[half, side],
                    sems[1],
                    half * 2 + side,
                    axes[half],
                    peer,
                )
            )
    for side in range(2):
        for half in range(2):
            _, right, left, _ = rings[half]
            step = 1 + side
            swaps[half, step].wait_recv()
            make(held.at[half, step], near.at[half, step], half, core, big_at(half, step))
            first[half, side].wait_recv()
            part = held.at[half, step, pl.ds(2 * side, 2)]
            part[...] = (
                part[...].astype(jnp.float32) + early[half, side].astype(jnp.float32)
            ).astype(jnp.bfloat16)
            second[half, side] = go(
                push(
                    held.at[half, step],
                    late.at[half, side],
                    sems[2],
                    half * 2 + side,
                    axes[half],
                    (right, left)[side],
                )
            )
    hook(1)
    for half in range(2):
        swaps[half, 3].wait_recv()
        make(held.at[half, 3], near.at[half, 3], half, core, big_at(half, 3))

    def small_at(half, step):
        me, right, left, far = rings[1 - half]
        return (far, right, left, me)[step]

    third = {}
    fourth = {}

    def gather_small(half, step):
        at = small_at(half, step)
        total[half, step] = (
            held[half, 3, at].astype(jnp.float32)
            + late[half, 0, at].astype(jnp.float32)
            + late[half, 1, at].astype(jnp.float32)
        ).astype(jnp.bfloat16)

    for half in range(2):
        _, right, left, _ = rings[1 - half]
        for side in range(2):
            second[half, side].wait_recv()
        gather_small(half, 0)
        for side, peer in ((0, right), (1, left)):
            third[half, side] = go(
                push(
                    total.at[half, 0, pl.ds(16 * side, 16)],
                    early_two.at[half, side],
                    sems[3],
                    half * 2 + side,
                    axes[1 - half],
                    peer,
                )
            )
        gather_small(half, 1)
        gather_small(half, 2)
    for side in range(2):
        for half in range(2):
            _, right, left, _ = rings[1 - half]
            third[half, side].wait_recv()
            part = total.at[half, 1 + side, pl.ds(16 * side, 16)]
            part[...] = (
                part[...].astype(jnp.float32) + early_two[half, side].astype(jnp.float32)
            ).astype(jnp.bfloat16)
            fourth[half, side] = go(
                push(
                    total.at[half, 1 + side],
                    late_two.at[half, side],
                    sems[4],
                    half * 2 + side,
                    axes[1 - half],
                    (right, left)[side],
                )
            )
    for half in range(2):
        at = small_at(half, 3)
        for side in range(2):
            fourth[half, side].wait_recv()
        finish(
            half,
            held[half, 3, at].astype(jnp.float32)
            + late[half, 0, at].astype(jnp.float32)
            + late[half, 1, at].astype(jnp.float32)
            + late_two[half, 0].astype(jnp.float32)
            + late_two[half, 1].astype(jnp.float32),
        )
    for copy in copies:
        copy.wait_send()


def scatter_scratch(width):
    return [
        pltpu.VMEM((2, 4, 4, HALF, width), jnp.bfloat16),
        pltpu.VMEM((2, 4, 4, HALF, width), jnp.bfloat16),
        pltpu.VMEM((2, 4, 4, HALF, width), jnp.bfloat16),
        pltpu.VMEM((2, 2, 2, HALF, width), jnp.bfloat16),
        pltpu.VMEM((2, 2, 4, HALF, width), jnp.bfloat16),
        pltpu.VMEM((2, 2, 16, width), jnp.bfloat16),
        pltpu.VMEM((2, 2, HALF, width), jnp.bfloat16),
        pltpu.VMEM((2, 3, HALF, width), jnp.bfloat16),
    ] + [pltpu.SemaphoreType.DMA((n,)) for n in (8, 8, 4, 4, 4, 4, 4, 4, 4, 4)]


def scatter_scope(left_ref, right_ref, scratch, finish, hook=lambda at: None):
    width = right_ref.shape[1]
    depth = right_ref.shape[0]
    tile = 512
    other, held, near, early, late, early_two, late_two, total = scratch[:8]
    flat = scratch[8:]
    sems = [(flat[2 * i], flat[2 * i + 1]) for i in range(5)]

    def make(dst, add, half, core, big):
        if half == 0:
            rows = left_ref[core, big, :, 0:HALF, :]
        else:
            rows = left_ref[core, :, big, HALF:ROWS, :]
        rows = rows.reshape(4 * HALF, depth)

        def column(i, carry):
            cols = pl.ds(pl.multiple_of(i * tile, tile), tile)
            value = jnp.dot(rows, right_ref[:, cols], preferred_element_type=jnp.float32)
            value = value.reshape(4, HALF, tile)
            if add is not None:
                value = value + add[:, :, cols].astype(jnp.float32)
            dst[:, :, cols] = value.astype(jnp.bfloat16)
            return carry

        lax.fori_loop(0, width // tile, column, 0)

    scatter_steps(
        make, other, held, near, early, late, early_two, late_two, total, sems, finish, hook
    )


def mix_kernel(
    left_ref, right_ref, base_ref, gain_ref, part_ref, res_ref, normed_ref, full_ref, *scratch
):
    meet(True)
    spread = Spread(part_ref, full_ref, paired(scratch[18:]))
    spread.send()

    def hook(at):
        if at == 0:
            spread.along()
        else:
            spread.relay()

    def finish(half, value):
        rows = pl.ds(half * HALF, HALF)
        value = value + base_ref[rows, :].astype(jnp.float32)
        res_ref[rows, :] = value
        scaling = lax.rsqrt(jnp.mean(value * value, axis=-1, keepdims=True) + EPSILON)
        normed_ref[rows, :] = (value * scaling * gain_ref[...]).astype(jnp.bfloat16)

    scatter_scope(left_ref, right_ref, scratch[:18], finish, hook)
    spread.arrive()
    spread.done()


def down_kernel(left_ref, right_ref, base_ref, out_ref, *scratch):
    meet()

    def finish(half, value):
        rows = pl.ds(half * HALF, HALF)
        out_ref[rows, :] = (value + base_ref[rows, :]).astype(jnp.bfloat16)

    scatter_scope(left_ref, right_ref, scratch, finish)


VM = pl.BlockSpec(memory_space=pltpu.VMEM)


def remote_params(number):
    return pltpu.CompilerParams(
        collective_id=number, has_side_effects=True, vmem_limit_bytes=60 * 1024 * 1024
    )


def mix(left, right, base, gain, parts):
    width = right.shape[1]
    return pl.pallas_call(
        mix_kernel,
        in_specs=[VM] * 5,
        out_specs=[VM] * 3,
        out_shape=[
            jax.ShapeDtypeStruct((ROWS, width), jnp.float32),
            jax.ShapeDtypeStruct((ROWS, width), jnp.bfloat16),
            jax.ShapeDtypeStruct((16, 4) + parts.shape[1:], jnp.bfloat16),
        ],
        scratch_shapes=scatter_scratch(width) + spread_sems(),
        compiler_params=remote_params(1),
        name="mix",
    )(left.reshape(2, 4, 4, ROWS, -1), right, base, gain.reshape(1, width), parts)


def down(left, right, base):
    width = right.shape[1]
    return pl.pallas_call(
        down_kernel,
        in_specs=[VM] * 3,
        out_specs=VM,
        out_shape=jax.ShapeDtypeStruct((ROWS, width), jnp.bfloat16),
        scratch_shapes=scatter_scratch(width),
        compiler_params=remote_params(2),
        name="down",
    )(left.reshape(2, 4, 4, ROWS, -1), right, base)


def gather_steps(x_ref, buf, sems, use, hook):
    core = lax.axis_index("core")
    axes = ("z", "x")
    rings = (ring("z"), ring("x"))
    copies = []

    def go(copy):
        copy.start()
        copies.append(copy)
        return copy

    def spot(half, big, small, c=None):
        return buf.at[half, big, core if c is None else c, small]

    one = {}
    cores = {}
    for half in range(2):
        big = rings[half][0]
        me, right, left, _ = rings[1 - half]
        buf[half, big, core, me] = x_ref[half * HALF : (half + 1) * HALF, :]
        for side, peer in ((0, right), (1, left)):
            one[half, side] = go(
                push(
                    x_ref.at[pl.ds(half * HALF, HALF)],
                    spot(half, big, me),
                    sems[0],
                    half * 2 + side,
                    axes[1 - half],
                    peer,
                )
            )
        cores[half, 0] = go(
            push(
                x_ref.at[pl.ds(half * HALF, HALF)],
                spot(half, big, me),
                sems[1],
                half * 4,
                "core",
                1 - core,
            )
        )
    hook(0)
    two = {}
    for half in range(2):
        big = rings[half][0]
        me, right, left, far = rings[1 - half]
        for side, (frm, to) in ((0, (left, right)), (1, (right, left))):
            one[half, side].wait_recv()
            piece = buf.at[half, big, core, frm, pl.ds(16 * side, 16)]
            two[half, side] = go(
                push(piece, piece, sems[2], half * 2 + side, axes[1 - half], to)
            )
            whole = spot(half, big, frm)
            cores[half, 1 + side] = go(
                push(whole, whole, sems[1], half * 4 + 1 + side, "core", 1 - core)
            )
    hook(1)
    three = {}
    for half in range(2):
        big, right, left, _ = rings[half]
        far = rings[1 - half][3]
        for side in range(2):
            two[half, side].wait_recv()
        whole = spot(half, big, far)
        chunk = buf.at[half, big, core]
        for side, peer in ((0, right), (1, left)):
            three[half, side] = go(
                push(chunk, chunk, sems[3], half * 2 + side, axes[half], peer)
            )
        cores[half, 3] = go(push(whole, whole, sems[1], half * 4 + 3, "core", 1 - core))
    hook(2)
    for half in range(2):
        for i in range(4):
            cores[half, i].wait_recv()
        use(half, rings[half][0])
    four = {}
    fives = {}
    for half in range(2):
        big, right, left, far = rings[half]
        for side, (frm, to) in ((0, (left, right)), (1, (right, left))):
            three[half, side].wait_recv()
            piece = buf.at[half, frm, core, pl.ds(2 * side, 2)]
            four[half, side] = go(push(piece, piece, sems[4], half * 2 + side, axes[half], to))
            chunk = buf.at[half, frm, core]
            fives[half, side] = go(
                push(chunk, chunk, sems[5], half * 4 + side, "core", 1 - core)
            )
    for half in range(2):
        _, right, left, _ = rings[half]
        for side, frm in ((0, left), (1, right)):
            fives[half, side].wait_recv()
            use(half, frm)
    for half in range(2):
        far = rings[half][3]
        for side in range(2):
            four[half, side].wait_recv()
            piece = buf.at[half, far, core, pl.ds(2 * side, 2)]
            fives[half, 2 + side] = go(
                push(piece, piece, sems[5], half * 4 + 2 + side, "core", 1 - core)
            )
    for half in range(2):
        for side in range(2):
            fives[half, 2 + side].wait_recv()
        use(half, rings[half][3])
    for copy in copies:
        copy.wait_send()


def gather_scratch(width):
    return [pltpu.VMEM((2, 4, 2, 4, HALF, width), jnp.bfloat16)] + [
        pltpu.SemaphoreType.DMA((n,)) for n in (4, 4, 8, 8, 4, 4, 4, 4, 4, 4, 8, 8)
    ]


def gather_scope(x_ref, scratch, use, hook=lambda at: None):
    buf = scratch[0]
    sems = [(scratch[1 + 2 * i], scratch[2 + 2 * i]) for i in range(6)]
    gather_steps(x_ref, buf, sems, use, hook)


def project_kernel(x_ref, part_ref, cos_ref, sin_ref, q_ref, kv_ref, full_ref, *scratch):
    meet(True)
    buf = scratch[0]
    spread = Spread(part_ref, full_ref, paired(scratch[13:19]))
    sems = paired(scratch[19:23])
    y, right, left, far = ring_y()
    width = x_ref.shape[1]
    started, passed, copies = [], [], []

    def hook(at):
        if at == 0:
            spread.send()
        elif at == 1:
            spread.along()
        else:
            spread.relay()
            spread.arrive()

    def window(half, big):
        if half == 0:
            return (slice(None), big, slice(None), pl.ds(0, HALF), slice(None))
        return (slice(None), slice(None), big, pl.ds(HALF, HALF), slice(None))

    def flip(value):
        return jnp.concatenate([value[:, HD // 2 :], value[:, : HD // 2]], axis=1)

    def forward(limit):
        while len(passed) < limit:
            index = len(passed)
            half, big, pushes = started[index]
            now = []
            for side, (frm, to) in ((0, (left, right)), (1, (right, left))):
                pushes[side].wait_recv()
                piece = kv_ref.at[(frm, side) + window(half, big)]
                copy = push(piece, piece, sems[1], index * 2 + side, None, at_y(to))
                copy.start()
                copies.append(copy)
                now.append(copy)
            passed.append(now)

    def use(half, big):
        rows = buf[half, big].reshape(8 * HALF, width)
        value = jnp.dot(
            rows, full_ref[...].reshape(width, 3 * 128), preferred_element_type=jnp.float32
        )
        at = window(half, big)
        cosine = cos_ref[at].reshape(8 * HALF, HD)
        sine = sin_ref[at].reshape(8 * HALF, HD)
        shape = (2, 4, HALF, HD)
        query = value[:, 0:HD]
        key = value[:, 128 : 128 + HD]
        q_ref[at] = (query * cosine + flip(query) * sine).astype(jnp.bfloat16).reshape(shape)
        kv_ref[(y, 0) + at] = (
            (key * cosine + flip(key) * sine).astype(jnp.bfloat16).reshape(shape)
        )
        kv_ref[(y, 1) + at] = value[:, 256 : 256 + HD].astype(jnp.bfloat16).reshape(shape)
        index = len(started)
        pushes = []
        for side, peer in ((0, right), (1, left)):
            piece = kv_ref.at[(y, slice(None)) + at]
            copy = push(piece, piece, sems[0], index * 2 + side, None, at_y(peer))
            copy.start()
            copies.append(copy)
            pushes.append(copy)
        started.append((half, big, pushes))
        forward(index)

    gather_scope(x_ref, scratch[:13], use, hook)
    forward(8)
    for now in passed:
        for copy in now:
            copy.wait_recv()
    for copy in copies:
        copy.wait_send()
    spread.done()


def lift_kernel(x_ref, w_ref, out_ref, *scratch):
    meet()
    buf = scratch[0]
    units = out_ref.shape[-1]

    def use(half, big):
        rows = buf[half, big].reshape(8 * HALF, x_ref.shape[1])
        value = jnp.dot(rows, w_ref[...], preferred_element_type=jnp.float32)
        gate, up = value[:, :units], value[:, units:]
        value = (gate / (1.0 + jnp.exp(-gate)) * up).astype(jnp.bfloat16)
        value = value.reshape(2, 4, HALF, units)
        if half == 0:
            out_ref[:, big, :, 0:HALF, :] = value
        else:
            out_ref[:, :, big, HALF:ROWS, :] = value

    gather_scope(x_ref, scratch, use)


def project(x, parts, cosine, sine):
    shape = (2, 4, 4, ROWS, HD)
    return pl.pallas_call(
        project_kernel,
        in_specs=[VM] * 4,
        out_specs=[VM] * 2,
        out_shape=[
            jax.ShapeDtypeStruct(shape, jnp.bfloat16),
            jax.ShapeDtypeStruct((4, 2) + shape, jnp.bfloat16),
        ],
        scratch_shapes=[pltpu.VMEM((16, 4) + parts.shape[1:], jnp.bfloat16)]
        + gather_scratch(x.shape[1])
        + spread_sems()
        + [pltpu.SemaphoreType.DMA((16,)) for _ in range(4)],
        compiler_params=remote_params(3),
        name="project",
    )(x, parts, cosine.reshape(shape), sine.reshape(shape))


def lift(x, w):
    units = w.shape[1] // 2
    return pl.pallas_call(
        lift_kernel,
        in_specs=[VM] * 2,
        out_specs=VM,
        out_shape=jax.ShapeDtypeStruct((2, 4, 4, ROWS, units), jnp.bfloat16),
        scratch_shapes=gather_scratch(x.shape[1]),
        compiler_params=remote_params(4),
        name="lift",
    )(x, w).reshape(32 * ROWS, units)


def rope_tables(positions):
    inverse = 1.0 / ROPE_BASE ** (jnp.arange(0, HD, 2).astype(jnp.float32) / HD)
    angles = positions.astype(jnp.float32)[:, None] * inverse[None, :]
    cosine, sine = jnp.cos(angles), jnp.sin(angles)
    return (
        jnp.concatenate([cosine, cosine], axis=-1),
        jnp.concatenate([-sine, sine], axis=-1),
    )


def body(
    states,
    attention_gain,
    forward_gain,
    attention_in,
    attention_out,
    gate_up,
    down_weight,
    block_map,
    prompt_lengths,
):
    width = states.shape[1]
    units = down_weight.shape[0]
    core = lax.axis_index("core")
    y_hi = lax.axis_index("y_hi")
    y_lo = lax.axis_index("y_lo")
    blocks = block_map.shape[0]
    long_blocks = blocks - SHORT_BLOCKS
    rows = 32 * ROWS

    swap = [
        (((a * 2 + c) * 2 + b), (((1 - a) * 2 + (1 - c)) * 2 + (1 - b)))
        for a in range(2)
        for c in range(2)
        for b in range(2)
        if b != c
    ]

    quarter = HD // 2

    def parts_of(weight, sections):
        piece = lax.dynamic_slice_in_dim(weight, y_lo * quarter, quarter, 0)
        piece = piece.reshape(quarter, sections, 16, 2, -1)
        piece = lax.dynamic_index_in_dim(piece, core, 3, keepdims=False).astype(jnp.bfloat16)
        return jnp.transpose(piece, (2, 0, 1, 3))

    qkv_parts = jnp.pad(parts_of(attention_in, 3), ((0, 0), (0, 0), (0, 0), (0, 128 - HD)))
    qkv_parts = qkv_parts.reshape(16, quarter, 3 * 128)
    gu_parts = parts_of(gate_up, 2).reshape(16, quarter, 2 * units)

    def own(shard):
        narrow = shard.astype(jnp.bfloat16)
        other = lax.ppermute(narrow, ("y_lo", "core", "y_hi"), swap)
        return jnp.where(y_hi == core, narrow, other)

    w_out = own(attention_out)
    w_down = own(down_weight)

    own_map = lax.dynamic_slice_in_dim(block_map, y_lo * 8, 8)
    at = jnp.arange(256, dtype=jnp.int32)
    at = (at // ROWS) * (2 * ROWS) + at % ROWS
    offset = at + y_hi * ROWS
    positions = jnp.where(
        own_map[:, None] < long_blocks, own_map[:, None] * BLOCK + offset[None], offset % SHORT_LEN
    ).reshape(-1)
    cosine, sine = rope_tables(positions)
    q, kv_all = project(rms_norm(states, attention_gain), qkv_parts, cosine, sine)

    offsets = jnp.concatenate([at, at + ROWS])
    prompt = (own_map - long_blocks)[:, None] * (BLOCK // SHORT_LEN) + offsets[None] // SHORT_LEN
    matches = prompt[:, :, None] == jnp.arange(prompt_lengths.shape[0], dtype=jnp.int32)
    length = jnp.sum(jnp.where(matches, prompt_lengths, 0), axis=2)
    live = (offsets[None] % SHORT_LEN < length).astype(jnp.float32)[:, None, :]

    places = jnp.stack([y_hi, y_lo]).astype(jnp.int32)
    attended = attention(
        q.reshape(8, 256, HD),
        kv_all.reshape(4, 2, 8, 256, HD),
        own_map,
        inverse_map(block_map),
        places,
        live,
    ).reshape(rows, HD)

    group = lax.dynamic_index_in_dim(
        kv_all.reshape(2, 2, 2, 2, 4, 4, ROWS, HD), y_lo, 1, False
    )

    def cache_rows(target):
        picked = lax.dynamic_index_in_dim(group, target, 2, False)
        return jnp.transpose(picked, (1, 2, 3, 0, 4, 5)).reshape(2, rows, HD)

    partner = lax.ppermute(
        cache_rows(1 - core),
        ("core", "y_hi"),
        [(b * 2 + b, (1 - b) * 2 + b) for b in range(2)],
    )
    cache = jnp.where(core == y_hi, cache_rows(core), partner)

    residual, normed_two, w_gu = mix(attended, w_out, states, forward_gain, gu_parts)
    activated = lift(normed_two, w_gu.reshape(width, 2 * units))
    hidden_out = down(activated, w_down, residual)
    return (hidden_out, cache[0], cache[1])


def solution(mesh):
    fine = Mesh(mesh.devices.reshape(2, 2, 4, 4, 2), ("y_lo", "core", "z", "x", "y_hi"))
    hid = ("z", "x", "y_hi")
    grp = ("y_lo", "core")
    in_specs = (
        P(grp + hid, None),
        P(),
        P(),
        P(hid, None),
        P(hid, None),
        P(hid, None),
        P(hid, None),
        P(),
        P(),
    )
    out_specs = (P(grp + hid, None), P(grp, hid), P(grp, hid))
    return jax.shard_map(
        body, mesh=fine, in_specs=in_specs, out_specs=out_specs, check_vma=False
    )
```

```python
import functools

import jax
import jax.numpy as jnp
import numpy as np
from jax import lax
from jax.experimental import pallas as pl
from jax.experimental.pallas import tpu as pltpu
from jax.sharding import Mesh, PartitionSpec as P

HD = 96
BLOCK = 512
SHORT_LEN = 32
WINDOW = 4096
SINKS = 4
SHORT_BLOCKS = 2
EPSILON = 1e-05
ROPE_BASE = 10000.0
MASK_FLOOR = -1e30
LOG2E = 1.4426950408889634

ROWS = 64
PLANE = ("core", "z", "x")


def rms_norm(values, gain):
    widened = values.astype(jnp.float32)
    scaling = lax.rsqrt(jnp.mean(widened * widened, axis=-1, keepdims=True) + EPSILON)
    return (widened * scaling * gain).astype(jnp.bfloat16)


def inverse_map(block_map):
    numbers = jnp.arange(block_map.shape[0], dtype=jnp.int32)
    matches = block_map[None, :] == numbers[:, None]
    return jnp.sum(jnp.where(matches, numbers[None, :], 0), axis=1)


def attention_kernel(
    own_map, slot_of, half_ref, q_ref, kv_ref, live_ref, o_ref, m_ref, l_ref, acc_ref
):
    step = pl.program_id(0)
    logical = own_map[step]
    own_half = half_ref[0]
    own_lo = half_ref[1]
    scale = HD ** (-0.5) * LOG2E
    rows = q_ref.shape[1]
    q = q_ref[0]

    row_at = lax.broadcasted_iota(jnp.int32, (rows, 2 * rows), 0)
    col_at = lax.broadcasted_iota(jnp.int32, (rows, 2 * rows), 1)
    row_off = (row_at // ROWS) * (2 * ROWS) + own_half * ROWS + row_at % ROWS
    col_in = col_at % rows
    col_off = (col_in // ROWS) * (2 * ROWS) + (col_at // rows) * ROWS + col_in % ROWS

    def pair(slot):
        low = slot // 8
        inner = slot % 8
        keys = jnp.concatenate([kv_ref[low, 0, inner], kv_ref[low + 2, 0, inner]], axis=0)
        values = jnp.concatenate([kv_ref[low, 1, inner], kv_ref[low + 2, 1, inner]], axis=0)
        return keys, values

    def scores_of(keys):
        return (
            lax.dot_general(
                q, keys, (((1,), (1,)), ((), ())), preferred_element_type=jnp.float32
            )
            * scale
        )

    def first(scores, values):
        peak = jnp.max(scores, axis=1, keepdims=True)
        weights = jnp.exp2(scores - peak)
        m_ref[...] = peak
        l_ref[...] = jnp.sum(weights, axis=1, keepdims=True)
        acc_ref[...] = jnp.dot(
            weights.astype(jnp.bfloat16), values, preferred_element_type=jnp.float32
        )

    def more(scores, values):
        old = m_ref[...]
        peak = jnp.maximum(old, jnp.max(scores, axis=1, keepdims=True))
        fade = jnp.exp2(old - peak)
        weights = jnp.exp2(scores - peak)
        m_ref[...] = peak
        l_ref[...] = l_ref[...] * fade + jnp.sum(weights, axis=1, keepdims=True)
        acc_ref[...] = acc_ref[...] * fade + jnp.dot(
            weights.astype(jnp.bfloat16), values, preferred_element_type=jnp.float32
        )

    is_long = logical < slot_of.shape[0] - SHORT_BLOCKS
    own_slot = own_lo * 8 + step

    @pl.when(jnp.logical_not(is_long))
    def _():
        keys, values = pair(own_slot)
        allowed = (row_off // SHORT_LEN == col_off // SHORT_LEN) & (col_off <= row_off)
        allowed = allowed & (live_ref[0] > 0.0)
        first(jnp.where(allowed, scores_of(keys), MASK_FLOOR), values)

    @pl.when(is_long)
    def _():
        keys, values = pair(own_slot)
        first(jnp.where(col_off <= row_off, scores_of(keys), MASK_FLOOR), values)
        span = WINDOW // BLOCK
        oldest = jnp.maximum(logical - span + 1, 0)

        def whole(index, carry):
            keys, values = pair(slot_of[index])
            more(scores_of(keys), values)
            return carry

        lax.fori_loop(oldest, logical, whole, 0)

        @pl.when(logical >= span)
        def _():
            edge = logical - span
            keys, values = pair(slot_of[edge])
            allowed = (col_off > row_off) | (edge * BLOCK + col_off < SINKS)
            more(jnp.where(allowed, scores_of(keys), MASK_FLOOR), values)

        @pl.when(logical > span)
        def _():
            slot = slot_of[0]
            keys = kv_ref[slot // 8, 0, slot % 8, 0:128]
            values = kv_ref[slot // 8, 1, slot % 8, 0:128]
            allowed = lax.broadcasted_iota(jnp.int32, (rows, 128), 1) < SINKS
            more(jnp.where(allowed, scores_of(keys), MASK_FLOOR), values)

    o_ref[0] = (acc_ref[...] / l_ref[...]).astype(jnp.bfloat16)


def attention(q, kv, own_map, slot_of, places, live):
    slots, rows, _ = q.shape
    return pl.pallas_call(
        attention_kernel,
        grid_spec=pltpu.PrefetchScalarGridSpec(
            num_scalar_prefetch=3,
            grid=(slots,),
            in_specs=[
                pl.BlockSpec((1, rows, HD), lambda i, *_: (i, 0, 0)),
                pl.BlockSpec(kv.shape, lambda i, *_: (0, 0, 0, 0, 0)),
                pl.BlockSpec((1, 1, 2 * rows), lambda i, *_: (i, 0, 0)),
            ],
            out_specs=pl.BlockSpec((1, rows, HD), lambda i, *_: (i, 0, 0)),
            scratch_shapes=[
                pltpu.VMEM((rows, 1), jnp.float32),
                pltpu.VMEM((rows, 1), jnp.float32),
                pltpu.VMEM((rows, HD), jnp.float32),
            ],
        ),
        out_shape=jax.ShapeDtypeStruct(q.shape, jnp.bfloat16),
        cost_estimate=pl.CostEstimate(
            flops=8_000_000_000, bytes_accessed=8_000_000, transcendentals=8_000_000
        ),
        name="attention",
    )(own_map, slot_of, places, q, kv, live)


MESH = pl.DeviceIdType.MESH
HALF = ROWS // 2


def ring(axis):
    me = lax.axis_index(axis)
    return me, lax.rem(me + 1, 4), lax.rem(me + 3, 4), lax.rem(me + 2, 4)


def ring_y():
    me = lax.axis_index("y_hi") * 2 + lax.axis_index("y_lo")
    return me, lax.rem(me + 1, 4), lax.rem(me + 3, 4), lax.rem(me + 2, 4)


def at_y(y):
    return {"y_hi": lax.div(y, 2), "y_lo": lax.rem(y, 2)}


def at_offset(offset):
    z, x = lax.axis_index("z"), lax.axis_index("x")
    return {"z": lax.rem(z + offset // 4, 4), "x": lax.rem(x + offset % 4, 4)}


def meet(whole=False):
    barrier = pltpu.get_barrier_semaphore()
    peers = [{"core": 1 - lax.axis_index("core")}]
    if whole:
        peers += [at_offset(offset) for offset in range(1, 16)]
        peers += [at_y(y) for y in ring_y()[1:3]]
    else:
        for axis in ("x", "z"):
            peers += [{axis: peer} for peer in ring(axis)[1:3]]
    for peer in peers:
        pl.semaphore_signal(barrier, inc=1, device_id=peer, device_id_type=MESH)
    pl.semaphore_wait(barrier, len(peers))


def push(src, dst, sems, at, axis, peer):
    send, recv = sems
    place = peer if axis is None else {axis: peer}
    return pltpu.make_async_remote_copy(
        src_ref=src,
        dst_ref=dst,
        send_sem=send.at[at],
        recv_sem=recv.at[at],
        device_id=place,
        device_id_type=MESH,
    )


class Spread:
    def __init__(self, parts, full, sems):
        self.parts, self.full, self.sems = parts, full, sems
        self.copies = []

    def go(self, copy):
        copy.start()
        self.copies.append(copy)
        return copy

    def send(self):
        me = lax.axis_index("z") * 4 + lax.axis_index("x")
        y = ring_y()[0]
        self.full[me, y] = self.parts[me]
        self.one = []
        for offset in range(1, 16):
            place = at_offset(offset)
            self.one.append(
                self.go(
                    push(
                        self.parts.at[place["z"] * 4 + place["x"]],
                        self.full.at[me, y],
                        self.sems[0],
                        offset,
                        None,
                        place,
                    )
                )
            )

    def along(self):
        for copy in self.one:
            copy.wait_recv()
        me, right, left, _ = ring_y()
        piece = self.full.at[:, me]
        self.two = [
            self.go(push(piece, piece, self.sems[1], side, None, at_y(peer)))
            for side, peer in ((0, right), (1, left))
        ]

    def relay(self):
        _, right, left, _ = ring_y()
        self.three = []
        for side, (frm, to) in ((0, (left, right)), (1, (right, left))):
            self.two[side].wait_recv()
            piece = self.full.at[pl.ds(8 * side, 8), frm]
            self.three.append(
                self.go(push(piece, piece, self.sems[2], side, None, at_y(to)))
            )

    def arrive(self):
        for copy in self.three:
            copy.wait_recv()

    def done(self):
        for copy in self.copies:
            copy.wait_send()


def spread_sems():
    return [pltpu.SemaphoreType.DMA((n,)) for n in (16, 16, 2, 2, 2, 2)]


def paired(flat):
    return [(flat[2 * i], flat[2 * i + 1]) for i in range(len(flat) // 2)]


def scatter_steps(
    make, other, held, near, early, late, early_two, late_two, total, sems, finish, hook
):
    core = lax.axis_index("core")
    rings = (ring("z"), ring("x"))
    axes = ("z", "x")
    copies = []

    def go(copy):
        copy.start()
        copies.append(copy)
        return copy

    def big_at(half, step):
        me, right, left, far = rings[half]
        return (far, right, left, me)[step]

    swaps = {}
    for step in range(4):
        for half in range(2):
            at = half * 4 + step
            make(other.at[half, step], None, half, 1 - core, big_at(half, step))
            swaps[half, step] = go(
                push(
                    other.at[half, step],
                    near.at[half, step],
                    sems[0],
                    at,
                    "core",
                    1 - core,
                )
            )

    hook(0)
    first = {}
    second = {}
    for half in range(2):
        _, right, left, _ = rings[half]
        swaps[half, 0].wait_recv()
        make(held.at[half, 0], near.at[half, 0], half, core, big_at(half, 0))
        for side, peer in ((0, right), (1, left)):
            first[half, side] = go(
                push(
                    held.at[half, 0, pl.ds(2 * side, 2)],
                    early.at[half, side],
                    sems[1],
                    half * 2 + side,
                    axes[half],
                    peer,
                )
            )
    for side in range(2):
        for half in range(2):
            _, right, left, _ = rings[half]
            step = 1 + side
            swaps[half, step].wait_recv()
            make(held.at[half, step], near.at[half, step], half, core, big_at(half, step))
            first[half, side].wait_recv()
            part = held.at[half, step, pl.ds(2 * side, 2)]
            part[...] = (
                part[...].astype(jnp.float32) + early[half, side].astype(jnp.float32)
            ).astype(jnp.bfloat16)
            second[half, side] = go(
                push(
                    held.at[half, step],
                    late.at[half, side],
                    sems[2],
                    half * 2 + side,
                    axes[half],
                    (right, left)[side],
                )
            )
    hook(1)
    for half in range(2):
        swaps[half, 3].wait_recv()
        make(held.at[half, 3], near.at[half, 3], half, core, big_at(half, 3))

    def small_at(half, step):
        me, right, left, far = rings[1 - half]
        return (far, right, left, me)[step]

    third = {}
    fourth = {}

    def gather_small(half, step):
        at = small_at(half, step)
        total[half, step] = (
            held[half, 3, at].astype(jnp.float32)
            + late[half, 0, at].astype(jnp.float32)
            + late[half, 1, at].astype(jnp.float32)
        ).astype(jnp.bfloat16)

    for half in range(2):
        _, right, left, _ = rings[1 - half]
        for side in range(2):
            second[half, side].wait_recv()
        gather_small(half, 0)
        for side, peer in ((0, right), (1, left)):
            third[half, side] = go(
                push(
                    total.at[half, 0, pl.ds(16 * side, 16)],
                    early_two.at[half, side],
                    sems[3],
                    half * 2 + side,
                    axes[1 - half],
                    peer,
                )
            )
        gather_small(half, 1)
        gather_small(half, 2)
    for side in range(2):
        for half in range(2):
            _, right, left, _ = rings[1 - half]
            third[half, side].wait_recv()
            part = total.at[half, 1 + side, pl.ds(16 * side, 16)]
            part[...] = (
                part[...].astype(jnp.float32) + early_two[half, side].astype(jnp.float32)
            ).astype(jnp.bfloat16)
            fourth[half, side] = go(
                push(
                    total.at[half, 1 + side],
                    late_two.at[half, side],
                    sems[4],
                    half * 2 + side,
                    axes[1 - half],
                    (right, left)[side],
                )
            )
    for half in range(2):
        at = small_at(half, 3)
        for side in range(2):
            fourth[half, side].wait_recv()
        finish(
            half,
            held[half, 3, at].astype(jnp.float32)
            + late[half, 0, at].astype(jnp.float32)
            + late[half, 1, at].astype(jnp.float32)
            + late_two[half, 0].astype(jnp.float32)
            + late_two[half, 1].astype(jnp.float32),
        )
    for copy in copies:
        copy.wait_send()


def scatter_scratch(width):
    return [
        pltpu.VMEM((2, 4, 4, HALF, width), jnp.bfloat16),
        pltpu.VMEM((2, 4, 4, HALF, width), jnp.bfloat16),
        pltpu.VMEM((2, 4, 4, HALF, width), jnp.bfloat16),
        pltpu.VMEM((2, 2, 2, HALF, width), jnp.bfloat16),
        pltpu.VMEM((2, 2, 4, HALF, width), jnp.bfloat16),
        pltpu.VMEM((2, 2, 16, width), jnp.bfloat16),
        pltpu.VMEM((2, 2, HALF, width), jnp.bfloat16),
        pltpu.VMEM((2, 3, HALF, width), jnp.bfloat16),
    ] + [pltpu.SemaphoreType.DMA((n,)) for n in (8, 8, 4, 4, 4, 4, 4, 4, 4, 4)]


def scatter_scope(left_ref, right_ref, scratch, finish, hook=lambda at: None):
    width = right_ref.shape[1]
    depth = right_ref.shape[0]
    tile = 512
    other, held, near, early, late, early_two, late_two, total = scratch[:8]
    flat = scratch[8:]
    sems = [(flat[2 * i], flat[2 * i + 1]) for i in range(5)]

    def make(dst, add, half, core, big):
        if half == 0:
            rows = left_ref[core, big, :, 0:HALF, :]
        else:
            rows = left_ref[core, :, big, HALF:ROWS, :]
        rows = rows.reshape(4 * HALF, depth)

        def column(i, carry):
            cols = pl.ds(pl.multiple_of(i * tile, tile), tile)
            value = jnp.dot(rows, right_ref[:, cols], preferred_element_type=jnp.float32)
            value = value.reshape(4, HALF, tile)
            if add is not None:
                value = value + add[:, :, cols].astype(jnp.float32)
            dst[:, :, cols] = value.astype(jnp.bfloat16)
            return carry

        lax.fori_loop(0, width // tile, column, 0)

    scatter_steps(
        make, other, held, near, early, late, early_two, late_two, total, sems, finish, hook
    )


def mix_kernel(
    left_ref, right_ref, base_ref, gain_ref, part_ref, res_ref, normed_ref, full_ref, *scratch
):
    meet(True)
    spread = Spread(part_ref, full_ref, paired(scratch[18:]))
    spread.send()

    def hook(at):
        if at == 0:
            spread.along()
        else:
            spread.relay()

    def finish(half, value):
        rows = pl.ds(half * HALF, HALF)
        value = value + base_ref[rows, :].astype(jnp.float32)
        res_ref[rows, :] = value
        scaling = lax.rsqrt(jnp.mean(value * value, axis=-1, keepdims=True) + EPSILON)
        normed_ref[rows, :] = (value * scaling * gain_ref[...]).astype(jnp.bfloat16)

    scatter_scope(left_ref, right_ref, scratch[:18], finish, hook)
    spread.arrive()
    spread.done()


def down_kernel(left_ref, right_ref, base_ref, out_ref, *scratch):
    meet()

    def finish(half, value):
        rows = pl.ds(half * HALF, HALF)
        out_ref[rows, :] = (value + base_ref[rows, :]).astype(jnp.bfloat16)

    scatter_scope(left_ref, right_ref, scratch, finish)


VM = pl.BlockSpec(memory_space=pltpu.VMEM)


def remote_params(number):
    return pltpu.CompilerParams(
        collective_id=number, has_side_effects=True, vmem_limit_bytes=60 * 1024 * 1024
    )


def mix(left, right, base, gain, parts):
    width = right.shape[1]
    return pl.pallas_call(
        mix_kernel,
        in_specs=[VM] * 5,
        out_specs=[VM] * 3,
        out_shape=[
            jax.ShapeDtypeStruct((ROWS, width), jnp.float32),
            jax.ShapeDtypeStruct((ROWS, width), jnp.bfloat16),
            jax.ShapeDtypeStruct((16, 4) + parts.shape[1:], jnp.bfloat16),
        ],
        scratch_shapes=scatter_scratch(width) + spread_sems(),
        compiler_params=remote_params(1),
        name="mix",
    )(left.reshape(2, 4, 4, ROWS, -1), right, base, gain.reshape(1, width), parts)


def down(left, right, base):
    width = right.shape[1]
    return pl.pallas_call(
        down_kernel,
        in_specs=[VM] * 3,
        out_specs=VM,
        out_shape=jax.ShapeDtypeStruct((ROWS, width), jnp.bfloat16),
        scratch_shapes=scatter_scratch(width),
        compiler_params=remote_params(2),
        name="down",
    )(left.reshape(2, 4, 4, ROWS, -1), right, base)


def gather_steps(x_ref, buf, sems, use, hook):
    core = lax.axis_index("core")
    axes = ("z", "x")
    rings = (ring("z"), ring("x"))
    copies = []

    def go(copy):
        copy.start()
        copies.append(copy)
        return copy

    def spot(half, big, small, c=None):
        return buf.at[half, big, core if c is None else c, small]

    one = {}
    cores = {}
    for half in range(2):
        big = rings[half][0]
        me, right, left, _ = rings[1 - half]
        buf[half, big, core, me] = x_ref[half * HALF : (half + 1) * HALF, :]
        for side, peer in ((0, right), (1, left)):
            one[half, side] = go(
                push(
                    x_ref.at[pl.ds(half * HALF, HALF)],
                    spot(half, big, me),
                    sems[0],
                    half * 2 + side,
                    axes[1 - half],
                    peer,
                )
            )
        cores[half, 0] = go(
            push(
                x_ref.at[pl.ds(half * HALF, HALF)],
                spot(half, big, me),
                sems[1],
                half * 4,
                "core",
                1 - core,
            )
        )
    hook(0)
    two = {}
    for half in range(2):
        big = rings[half][0]
        me, right, left, far = rings[1 - half]
        for side, (frm, to) in ((0, (left, right)), (1, (right, left))):
            one[half, side].wait_recv()
            piece = buf.at[half, big, core, frm, pl.ds(16 * side, 16)]
            two[half, side] = go(
                push(piece, piece, sems[2], half * 2 + side, axes[1 - half], to)
            )
            whole = spot(half, big, frm)
            cores[half, 1 + side] = go(
                push(whole, whole, sems[1], half * 4 + 1 + side, "core", 1 - core)
            )
    hook(1)
    three = {}
    for half in range(2):
        big, right, left, _ = rings[half]
        far = rings[1 - half][3]
        for side in range(2):
            two[half, side].wait_recv()
        whole = spot(half, big, far)
        chunk = buf.at[half, big, core]
        for side, peer in ((0, right), (1, left)):
            three[half, side] = go(
                push(chunk, chunk, sems[3], half * 2 + side, axes[half], peer)
            )
        cores[half, 3] = go(push(whole, whole, sems[1], half * 4 + 3, "core", 1 - core))
    hook(2)
    for half in range(2):
        for i in range(4):
            cores[half, i].wait_recv()
        use(half, rings[half][0])
    four = {}
    fives = {}
    for half in range(2):
        big, right, left, far = rings[half]
        for side, (frm, to) in ((0, (left, right)), (1, (right, left))):
            three[half, side].wait_recv()
            piece = buf.at[half, frm, core, pl.ds(2 * side, 2)]
            four[half, side] = go(push(piece, piece, sems[4], half * 2 + side, axes[half], to))
            chunk = buf.at[half, frm, core]
            fives[half, side] = go(
                push(chunk, chunk, sems[5], half * 4 + side, "core", 1 - core)
            )
    for half in range(2):
        _, right, left, _ = rings[half]
        for side, frm in ((0, left), (1, right)):
            fives[half, side].wait_recv()
            use(half, frm)
    for half in range(2):
        far = rings[half][3]
        for side in range(2):
            four[half, side].wait_recv()
            piece = buf.at[half, far, core, pl.ds(2 * side, 2)]
            fives[half, 2 + side] = go(
                push(piece, piece, sems[5], half * 4 + 2 + side, "core", 1 - core)
            )
    for half in range(2):
        for side in range(2):
            fives[half, 2 + side].wait_recv()
        use(half, rings[half][3])
    for copy in copies:
        copy.wait_send()


def gather_scratch(width):
    return [pltpu.VMEM((2, 4, 2, 4, HALF, width), jnp.bfloat16)] + [
        pltpu.SemaphoreType.DMA((n,)) for n in (4, 4, 8, 8, 4, 4, 4, 4, 4, 4, 8, 8)
    ]


def gather_scope(x_ref, scratch, use, hook=lambda at: None):
    buf = scratch[0]
    sems = [(scratch[1 + 2 * i], scratch[2 + 2 * i]) for i in range(6)]
    gather_steps(x_ref, buf, sems, use, hook)


def project_kernel(x_ref, part_ref, cos_ref, sin_ref, q_ref, kv_ref, full_ref, *scratch):
    meet(True)
    buf = scratch[0]
    spread = Spread(part_ref, full_ref, paired(scratch[13:19]))
    sems = paired(scratch[19:23])
    y, right, left, far = ring_y()
    width = x_ref.shape[1]
    started, passed, copies = [], [], []

    def hook(at):
        if at == 0:
            spread.send()
        elif at == 1:
            spread.along()
        else:
            spread.relay()
            spread.arrive()

    def window(half, big):
        if half == 0:
            return (slice(None), big, slice(None), pl.ds(0, HALF), slice(None))
        return (slice(None), slice(None), big, pl.ds(HALF, HALF), slice(None))

    def flip(value):
        return jnp.concatenate([value[:, HD // 2 :], value[:, : HD // 2]], axis=1)

    def forward(limit):
        while len(passed) < limit:
            index = len(passed)
            half, big, pushes = started[index]
            now = []
            for side, (frm, to) in ((0, (left, right)), (1, (right, left))):
                pushes[side].wait_recv()
                piece = kv_ref.at[(frm, side) + window(half, big)]
                copy = push(piece, piece, sems[1], index * 2 + side, None, at_y(to))
                copy.start()
                copies.append(copy)
                now.append(copy)
            passed.append(now)

    def use(half, big):
        rows = buf[half, big].reshape(8 * HALF, width)
        value = jnp.dot(
            rows, full_ref[...].reshape(width, 3 * 128), preferred_element_type=jnp.float32
        )
        at = window(half, big)
        cosine = cos_ref[at].reshape(8 * HALF, HD)
        sine = sin_ref[at].reshape(8 * HALF, HD)
        shape = (2, 4, HALF, HD)
        query = value[:, 0:HD]
        key = value[:, 128 : 128 + HD]
        q_ref[at] = (query * cosine + flip(query) * sine).astype(jnp.bfloat16).reshape(shape)
        kv_ref[(y, 0) + at] = (
            (key * cosine + flip(key) * sine).astype(jnp.bfloat16).reshape(shape)
        )
        kv_ref[(y, 1) + at] = value[:, 256 : 256 + HD].astype(jnp.bfloat16).reshape(shape)
        index = len(started)
        pushes = []
        for side, peer in ((0, right), (1, left)):
            piece = kv_ref.at[(y, slice(None)) + at]
            copy = push(piece, piece, sems[0], index * 2 + side, None, at_y(peer))
            copy.start()
            copies.append(copy)
            pushes.append(copy)
        started.append((half, big, pushes))
        forward(index)

    gather_scope(x_ref, scratch[:13], use, hook)
    forward(8)
    for now in passed:
        for copy in now:
            copy.wait_recv()
    for copy in copies:
        copy.wait_send()
    spread.done()


def lift_kernel(x_ref, w_ref, out_ref, *scratch):
    meet()
    buf = scratch[0]
    units = out_ref.shape[-1]

    def use(half, big):
        rows = buf[half, big].reshape(8 * HALF, x_ref.shape[1])
        value = jnp.dot(rows, w_ref[...], preferred_element_type=jnp.float32)
        gate, up = value[:, :units], value[:, units:]
        value = (gate / (1.0 + jnp.exp(-gate)) * up).astype(jnp.bfloat16)
        value = value.reshape(2, 4, HALF, units)
        if half == 0:
            out_ref[:, big, :, 0:HALF, :] = value
        else:
            out_ref[:, :, big, HALF:ROWS, :] = value

    gather_scope(x_ref, scratch, use)


def project(x, parts, cosine, sine):
    shape = (2, 4, 4, ROWS, HD)
    return pl.pallas_call(
        project_kernel,
        in_specs=[VM] * 4,
        out_specs=[VM] * 2,
        out_shape=[
            jax.ShapeDtypeStruct(shape, jnp.bfloat16),
            jax.ShapeDtypeStruct((4, 2) + shape, jnp.bfloat16),
        ],
        scratch_shapes=[pltpu.VMEM((16, 4) + parts.shape[1:], jnp.bfloat16)]
        + gather_scratch(x.shape[1])
        + spread_sems()
        + [pltpu.SemaphoreType.DMA((16,)) for _ in range(4)],
        compiler_params=remote_params(3),
        name="project",
    )(x, parts, cosine.reshape(shape), sine.reshape(shape))


def lift(x, w):
    units = w.shape[1] // 2
    return pl.pallas_call(
        lift_kernel,
        in_specs=[VM] * 2,
        out_specs=VM,
        out_shape=jax.ShapeDtypeStruct((2, 4, 4, ROWS, units), jnp.bfloat16),
        scratch_shapes=gather_scratch(x.shape[1]),
        compiler_params=remote_params(4),
        name="lift",
    )(x, w).reshape(32 * ROWS, units)


def rope_constants():
    inverse = 1.0 / ROPE_BASE ** (np.arange(0, HD, 2) / HD)

    def table(positions):
        angles = np.asarray(positions, np.float64)[:, None] * inverse[None, :]
        cosine, sine = np.cos(angles), np.sin(angles)
        return np.stack(
            [np.concatenate([cosine, cosine], 1), np.concatenate([-sine, sine], 1)]
        ).astype(np.float32)

    blocks = np.arange(16)
    base = table(np.where(blocks < 16 - SHORT_BLOCKS, blocks * BLOCK, 0))
    at = np.arange(256)
    at = (at // ROWS) * (2 * ROWS) + at % ROWS
    inner = np.stack(
        [
            np.stack([table(at + h * ROWS), table((at + h * ROWS) % SHORT_LEN)])
            for h in range(2)
        ]
    )
    return base[:, :, None, :], inner


PREP = 4


def prep_kernel(
    own_map,
    place,
    x_ref,
    gain_ref,
    *refs,
):
    wide = refs[:5]
    out_ref, down_ref, base_ref, inner_ref = refs[5:9]
    normed_ref, qkv_ref, gu_ref, wout_ref, wdown_ref, cos_ref, sin_ref = refs[9:]
    step = pl.program_id(0)
    core = place[1]
    normed_ref[...] = rms_norm(x_ref[...], gain_ref[...])
    wout_ref[...] = out_ref[...].astype(jnp.bfloat16)
    wdown_ref[...] = down_ref[...].astype(jnp.bfloat16)
    units = gu_ref.shape[2] // 2
    blank = jnp.zeros((qkv_ref.shape[1], 128 - HD), jnp.float32)
    for j in range(4):
        for k in range(2):
            cols = pl.ds(pl.multiple_of((2 * j + core) * units, 128), units)
            gu_ref[j, :, k * units : (k + 1) * units] = wide[3 + k][:, cols].astype(
                jnp.bfloat16
            )
        for k in range(3):
            even = wide[k][:, 2 * j * HD : (2 * j + 1) * HD]
            odd = wide[k][:, (2 * j + 1) * HD : (2 * j + 2) * HD]
            value = jnp.concatenate([jnp.where(core == 0, even, odd), blank], axis=1)
            qkv_ref[j, :, k * 128 : (k + 1) * 128] = value.astype(jnp.bfloat16)
    for j in range(2):
        logical = own_map[2 * step + j]
        kind = (logical >= base_ref.shape[1] - SHORT_BLOCKS).astype(jnp.int32)
        cos_at, sin_at = base_ref[0, logical], base_ref[1, logical]
        cos_in, sin_in = inner_ref[0, kind, 0], inner_ref[0, kind, 1]
        rows = pl.ds(j * 256, 256)
        cos_ref[rows, :] = cos_at * cos_in - sin_at * sin_in
        sin_ref[rows, :] = sin_at * cos_in + cos_at * sin_in


def prep(states, gain, attention_in, attention_out, gate_up, down_weight, own_map, place):
    width = states.shape[1]
    units = down_weight.shape[0]
    quarter = HD // 2
    base, inner = rope_constants()

    def wide(columns, section):
        return pl.BlockSpec(
            (quarter, columns), lambda i, own, at: (at[0], section * PREP + i)
        )

    def across(shape):
        return pl.BlockSpec(shape, lambda i, *_: (0, i))

    def along(shape):
        return pl.BlockSpec(shape, lambda i, *_: (i,) + (0,) * (len(shape) - 1))

    def whole(array):
        return pl.BlockSpec(array.shape, lambda i, *_: (0,) * array.ndim)

    gain = gain.reshape(1, width)
    rows = 32 * ROWS
    return pl.pallas_call(
        prep_kernel,
        grid_spec=pltpu.PrefetchScalarGridSpec(
            num_scalar_prefetch=2,
            grid=(PREP,),
            in_specs=[along((ROWS // PREP, width)), whole(gain)]
            + [wide(8 * HD, k) for k in range(3)]
            + [wide(8 * units, k) for k in range(2)]
            + [
                across((HD, width // PREP)),
                along((units // PREP, width)),
                whole(base),
                pl.BlockSpec(
                    (1,) + inner.shape[1:], lambda i, own, at: (at[2], 0, 0, 0, 0)
                ),
            ],
            out_specs=[
                along((ROWS // PREP, width)),
                along((16 // PREP, quarter, 3 * 128)),
                along((16 // PREP, quarter, 2 * units)),
                across((HD, width // PREP)),
                along((units // PREP, width)),
                along((rows // PREP, HD)),
                along((rows // PREP, HD)),
            ],
        ),
        out_shape=[
            jax.ShapeDtypeStruct((ROWS, width), jnp.bfloat16),
            jax.ShapeDtypeStruct((16, quarter, 3 * 128), jnp.bfloat16),
            jax.ShapeDtypeStruct((16, quarter, 2 * units), jnp.bfloat16),
            jax.ShapeDtypeStruct((HD, width), jnp.bfloat16),
            jax.ShapeDtypeStruct((units, width), jnp.bfloat16),
            jax.ShapeDtypeStruct((rows, HD), jnp.float32),
            jax.ShapeDtypeStruct((rows, HD), jnp.float32),
        ],
        compiler_params=pltpu.CompilerParams(vmem_limit_bytes=48 * 1024 * 1024),
        name="prep",
    )(
        own_map,
        place,
        states,
        gain,
        attention_in,
        attention_in,
        attention_in,
        gate_up,
        gate_up,
        attention_out,
        down_weight,
        base,
        inner,
    )


def body(
    states,
    attention_gain,
    forward_gain,
    attention_in,
    attention_out,
    gate_up,
    down_weight,
    block_map,
    prompt_lengths,
):
    width = states.shape[1]
    units = down_weight.shape[0]
    core = lax.axis_index("core")
    y_hi = lax.axis_index("y_hi")
    y_lo = lax.axis_index("y_lo")
    blocks = block_map.shape[0]
    long_blocks = blocks - SHORT_BLOCKS
    rows = 32 * ROWS

    swap = [
        (((a * 2 + c) * 2 + b), (((1 - a) * 2 + (1 - c)) * 2 + (1 - b)))
        for a in range(2)
        for c in range(2)
        for b in range(2)
        if b != c
    ]

    own_map = lax.dynamic_slice_in_dim(block_map, y_lo * 8, 8)
    normed, qkv_parts, gu_parts, w_out, w_down, cosine, sine = prep(
        states,
        attention_gain,
        attention_in,
        attention_out,
        gate_up,
        down_weight,
        own_map,
        jnp.stack([y_lo, core, y_hi]).astype(jnp.int32),
    )

    def own(narrow):
        other = lax.ppermute(narrow, ("y_lo", "core", "y_hi"), swap)
        return jnp.where(y_hi == core, narrow, other)

    w_out = own(w_out)
    w_down = own(w_down)

    at = jnp.arange(256, dtype=jnp.int32)
    at = (at // ROWS) * (2 * ROWS) + at % ROWS
    q, kv_all = project(normed, qkv_parts, cosine, sine)

    offsets = jnp.concatenate([at, at + ROWS])
    prompt = (own_map - long_blocks)[:, None] * (BLOCK // SHORT_LEN) + offsets[None] // SHORT_LEN
    matches = prompt[:, :, None] == jnp.arange(prompt_lengths.shape[0], dtype=jnp.int32)
    length = jnp.sum(jnp.where(matches, prompt_lengths, 0), axis=2)
    live = (offsets[None] % SHORT_LEN < length).astype(jnp.float32)[:, None, :]

    places = jnp.stack([y_hi, y_lo]).astype(jnp.int32)
    attended = attention(
        q.reshape(8, 256, HD),
        kv_all.reshape(4, 2, 8, 256, HD),
        own_map,
        inverse_map(block_map),
        places,
        live,
    ).reshape(rows, HD)

    group = lax.dynamic_index_in_dim(
        kv_all.reshape(2, 2, 2, 2, 4, 4, ROWS, HD), y_lo, 1, False
    )

    def cache_rows(target):
        picked = lax.dynamic_index_in_dim(group, target, 2, False)
        return jnp.transpose(picked, (1, 2, 3, 0, 4, 5)).reshape(2, rows, HD)

    partner = lax.ppermute(
        cache_rows(1 - core),
        ("core", "y_hi"),
        [(b * 2 + b, (1 - b) * 2 + b) for b in range(2)],
    )
    cache = jnp.where(core == y_hi, cache_rows(core), partner)

    residual, normed_two, w_gu = mix(attended, w_out, states, forward_gain, gu_parts)
    activated = lift(normed_two, w_gu.reshape(width, 2 * units))
    hidden_out = down(activated, w_down, residual)
    return (hidden_out, cache[0], cache[1])


def solution(mesh):
    fine = Mesh(mesh.devices.reshape(2, 2, 4, 4, 2), ("y_lo", "core", "z", "x", "y_hi"))
    hid = ("z", "x", "y_hi")
    grp = ("y_lo", "core")
    in_specs = (
        P(grp + hid, None),
        P(),
        P(),
        P(hid, None),
        P(hid, None),
        P(hid, None),
        P(hid, None),
        P(),
        P(),
    )
    out_specs = (P(grp + hid, None), P(grp, hid), P(grp, hid))
    return jax.shard_map(
        body, mesh=fine, in_specs=in_specs, out_specs=out_specs, check_vma=False
    )
```

```python
import functools

import jax
import jax.numpy as jnp
import numpy as np
from jax import lax
from jax.experimental import pallas as pl
from jax.experimental.pallas import tpu as pltpu
from jax.sharding import Mesh, PartitionSpec as P

HD = 96
BLOCK = 512
SHORT_LEN = 32
WINDOW = 4096
SINKS = 4
SHORT_BLOCKS = 2
EPSILON = 1e-05
ROPE_BASE = 10000.0
MASK_FLOOR = -1e30
LOG2E = 1.4426950408889634

ROWS = 64
PLANE = ("core", "z", "x")


def rms_norm(values, gain):
    widened = values.astype(jnp.float32)
    scaling = lax.rsqrt(jnp.mean(widened * widened, axis=-1, keepdims=True) + EPSILON)
    return (widened * scaling * gain).astype(jnp.bfloat16)


def inverse_map(block_map):
    numbers = jnp.arange(block_map.shape[0], dtype=jnp.int32)
    matches = block_map[None, :] == numbers[:, None]
    return jnp.sum(jnp.where(matches, numbers[None, :], 0), axis=1)


def attention_kernel(
    own_map, slot_of, half_ref, q_ref, kv_ref, live_ref, o_ref, m_ref, l_ref, acc_ref
):
    step = pl.program_id(0)
    logical = own_map[step]
    own_half = half_ref[0]
    own_lo = half_ref[1]
    scale = HD ** (-0.5) * LOG2E
    rows = q_ref.shape[1]
    q = q_ref[0]

    row_at = lax.broadcasted_iota(jnp.int32, (rows, 2 * rows), 0)
    col_at = lax.broadcasted_iota(jnp.int32, (rows, 2 * rows), 1)
    row_off = (row_at // ROWS) * (2 * ROWS) + own_half * ROWS + row_at % ROWS
    col_in = col_at % rows
    col_off = (col_in // ROWS) * (2 * ROWS) + (col_at // rows) * ROWS + col_in % ROWS

    def pair(slot):
        low = slot // 8
        inner = slot % 8
        keys = jnp.concatenate([kv_ref[low, 0, inner], kv_ref[low + 2, 0, inner]], axis=0)
        values = jnp.concatenate([kv_ref[low, 1, inner], kv_ref[low + 2, 1, inner]], axis=0)
        return keys, values

    def scores_of(keys):
        return (
            lax.dot_general(
                q, keys, (((1,), (1,)), ((), ())), preferred_element_type=jnp.float32
            )
            * scale
        )

    def first(scores, values):
        peak = jnp.max(scores, axis=1, keepdims=True)
        weights = jnp.exp2(scores - peak)
        m_ref[...] = peak
        l_ref[...] = jnp.sum(weights, axis=1, keepdims=True)
        acc_ref[...] = jnp.dot(
            weights.astype(jnp.bfloat16), values, preferred_element_type=jnp.float32
        )

    def more(scores, values):
        old = m_ref[...]
        peak = jnp.maximum(old, jnp.max(scores, axis=1, keepdims=True))
        fade = jnp.exp2(old - peak)
        weights = jnp.exp2(scores - peak)
        m_ref[...] = peak
        l_ref[...] = l_ref[...] * fade + jnp.sum(weights, axis=1, keepdims=True)
        acc_ref[...] = acc_ref[...] * fade + jnp.dot(
            weights.astype(jnp.bfloat16), values, preferred_element_type=jnp.float32
        )

    is_long = logical < slot_of.shape[0] - SHORT_BLOCKS
    own_slot = own_lo * 8 + step

    @pl.when(jnp.logical_not(is_long))
    def _():
        keys, values = pair(own_slot)
        allowed = (row_off // SHORT_LEN == col_off // SHORT_LEN) & (col_off <= row_off)
        allowed = allowed & (live_ref[0] > 0.0)
        first(jnp.where(allowed, scores_of(keys), MASK_FLOOR), values)

    @pl.when(is_long)
    def _():
        keys, values = pair(own_slot)
        first(jnp.where(col_off <= row_off, scores_of(keys), MASK_FLOOR), values)
        span = WINDOW // BLOCK
        oldest = jnp.maximum(logical - span + 1, 0)

        def whole(index, carry):
            keys, values = pair(slot_of[index])
            more(scores_of(keys), values)
            return carry

        lax.fori_loop(oldest, logical, whole, 0)

        @pl.when(logical >= span)
        def _():
            edge = logical - span
            keys, values = pair(slot_of[edge])
            allowed = (col_off > row_off) | (edge * BLOCK + col_off < SINKS)
            more(jnp.where(allowed, scores_of(keys), MASK_FLOOR), values)

        @pl.when(logical > span)
        def _():
            slot = slot_of[0]
            keys = kv_ref[slot // 8, 0, slot % 8, 0:128]
            values = kv_ref[slot // 8, 1, slot % 8, 0:128]
            allowed = lax.broadcasted_iota(jnp.int32, (rows, 128), 1) < SINKS
            more(jnp.where(allowed, scores_of(keys), MASK_FLOOR), values)

    o_ref[0] = (acc_ref[...] / l_ref[...]).astype(jnp.bfloat16)


def attention(q, kv, own_map, slot_of, places, live):
    slots, rows, _ = q.shape
    return pl.pallas_call(
        attention_kernel,
        grid_spec=pltpu.PrefetchScalarGridSpec(
            num_scalar_prefetch=3,
            grid=(slots,),
            in_specs=[
                pl.BlockSpec((1, rows, HD), lambda i, *_: (i, 0, 0)),
                pl.BlockSpec(kv.shape, lambda i, *_: (0, 0, 0, 0, 0)),
                pl.BlockSpec((1, 1, 2 * rows), lambda i, *_: (i, 0, 0)),
            ],
            out_specs=pl.BlockSpec((1, rows, HD), lambda i, *_: (i, 0, 0)),
            scratch_shapes=[
                pltpu.VMEM((rows, 1), jnp.float32),
                pltpu.VMEM((rows, 1), jnp.float32),
                pltpu.VMEM((rows, HD), jnp.float32),
            ],
        ),
        out_shape=jax.ShapeDtypeStruct(q.shape, jnp.bfloat16),
        cost_estimate=pl.CostEstimate(
            flops=8_000_000_000, bytes_accessed=8_000_000, transcendentals=8_000_000
        ),
        name="attention",
    )(own_map, slot_of, places, q, kv, live)


MESH = pl.DeviceIdType.MESH
HALF = ROWS // 2


def ring(axis):
    me = lax.axis_index(axis)
    return me, lax.rem(me + 1, 4), lax.rem(me + 3, 4), lax.rem(me + 2, 4)


def ring_y():
    me = lax.axis_index("y_hi") * 2 + lax.axis_index("y_lo")
    return me, lax.rem(me + 1, 4), lax.rem(me + 3, 4), lax.rem(me + 2, 4)


def at_y(y):
    return {"y_hi": lax.div(y, 2), "y_lo": lax.rem(y, 2)}


def at_offset(offset):
    z, x = lax.axis_index("z"), lax.axis_index("x")
    return {"z": lax.rem(z + offset // 4, 4), "x": lax.rem(x + offset % 4, 4)}


def meet(whole=False):
    barrier = pltpu.get_barrier_semaphore()
    peers = [{"core": 1 - lax.axis_index("core")}]
    if whole:
        peers += [at_offset(offset) for offset in range(1, 16)]
        peers += [at_y(y) for y in ring_y()[1:3]]
    else:
        for axis in ("x", "z"):
            peers += [{axis: peer} for peer in ring(axis)[1:3]]
    for peer in peers:
        pl.semaphore_signal(barrier, inc=1, device_id=peer, device_id_type=MESH)
    pl.semaphore_wait(barrier, len(peers))


def push(src, dst, sems, at, axis, peer):
    send, recv = sems
    place = peer if axis is None else {axis: peer}
    return pltpu.make_async_remote_copy(
        src_ref=src,
        dst_ref=dst,
        send_sem=send.at[at],
        recv_sem=recv.at[at],
        device_id=place,
        device_id_type=MESH,
    )


class Spread:
    def __init__(self, parts, full, sems):
        self.parts, self.full, self.sems = parts, full, sems
        self.copies = []

    def go(self, copy):
        copy.start()
        self.copies.append(copy)
        return copy

    def send(self):
        me = lax.axis_index("z") * 4 + lax.axis_index("x")
        y = ring_y()[0]
        self.full[me, y] = self.parts[me]
        self.one = []
        for offset in range(1, 16):
            place = at_offset(offset)
            self.one.append(
                self.go(
                    push(
                        self.parts.at[place["z"] * 4 + place["x"]],
                        self.full.at[me, y],
                        self.sems[0],
                        offset,
                        None,
                        place,
                    )
                )
            )

    def along(self):
        for copy in self.one:
            copy.wait_recv()
        me, right, left, _ = ring_y()
        piece = self.full.at[:, me]
        self.two = [
            self.go(push(piece, piece, self.sems[1], side, None, at_y(peer)))
            for side, peer in ((0, right), (1, left))
        ]

    def relay(self):
        _, right, left, _ = ring_y()
        self.three = []
        for side, (frm, to) in ((0, (left, right)), (1, (right, left))):
            self.two[side].wait_recv()
            piece = self.full.at[pl.ds(8 * side, 8), frm]
            self.three.append(
                self.go(push(piece, piece, self.sems[2], side, None, at_y(to)))
            )

    def arrive(self):
        for copy in self.three:
            copy.wait_recv()

    def done(self):
        for copy in self.copies:
            copy.wait_send()


def spread_sems():
    return [pltpu.SemaphoreType.DMA((n,)) for n in (16, 16, 2, 2, 2, 2)]


def paired(flat):
    return [(flat[2 * i], flat[2 * i + 1]) for i in range(len(flat) // 2)]


def scatter_steps(
    make, other, held, near, early, late, early_two, late_two, total, sems, finish, hook
):
    core = lax.axis_index("core")
    rings = (ring("z"), ring("x"))
    axes = ("z", "x")
    copies = []

    def go(copy):
        copy.start()
        copies.append(copy)
        return copy

    def big_at(half, step):
        me, right, left, far = rings[half]
        return (far, right, left, me)[step]

    swaps = {}

    def hand_over(step):
        for half in range(2):
            at = half * 4 + step
            make(other.at[half, step], None, half, 1 - core, big_at(half, step))
            swaps[half, step] = go(
                push(
                    other.at[half, step],
                    near.at[half, step],
                    sems[0],
                    at,
                    "core",
                    1 - core,
                )
            )

    hand_over(0)
    hand_over(1)
    first = {}
    second = {}
    for half in range(2):
        _, right, left, _ = rings[half]
        swaps[half, 0].wait_recv()
        make(held.at[half, 0], near.at[half, 0], half, core, big_at(half, 0))
        for side, peer in ((0, right), (1, left)):
            first[half, side] = go(
                push(
                    held.at[half, 0, pl.ds(2 * side, 2)],
                    early.at[half, side],
                    sems[1],
                    half * 2 + side,
                    axes[half],
                    peer,
                )
            )
    hand_over(2)
    hand_over(3)
    hook(0)
    for side in range(2):
        for half in range(2):
            _, right, left, _ = rings[half]
            step = 1 + side
            swaps[half, step].wait_recv()
            make(held.at[half, step], near.at[half, step], half, core, big_at(half, step))
            first[half, side].wait_recv()
            part = held.at[half, step, pl.ds(2 * side, 2)]
            part[...] = (
                part[...].astype(jnp.float32) + early[half, side].astype(jnp.float32)
            ).astype(jnp.bfloat16)
            second[half, side] = go(
                push(
                    held.at[half, step],
                    late.at[half, side],
                    sems[2],
                    half * 2 + side,
                    axes[half],
                    (right, left)[side],
                )
            )
    hook(1)
    for half in range(2):
        swaps[half, 3].wait_recv()
        make(held.at[half, 3], near.at[half, 3], half, core, big_at(half, 3))

    def small_at(half, step):
        me, right, left, far = rings[1 - half]
        return (far, right, left, me)[step]

    third = {}
    fourth = {}

    def gather_small(half, step):
        at = small_at(half, step)
        total[half, step] = (
            held[half, 3, at].astype(jnp.float32)
            + late[half, 0, at].astype(jnp.float32)
            + late[half, 1, at].astype(jnp.float32)
        ).astype(jnp.bfloat16)

    for half in range(2):
        _, right, left, _ = rings[1 - half]
        for side in range(2):
            second[half, side].wait_recv()
        gather_small(half, 0)
        for side, peer in ((0, right), (1, left)):
            third[half, side] = go(
                push(
                    total.at[half, 0, pl.ds(16 * side, 16)],
                    early_two.at[half, side],
                    sems[3],
                    half * 2 + side,
                    axes[1 - half],
                    peer,
                )
            )
        gather_small(half, 1)
        gather_small(half, 2)
    for side in range(2):
        for half in range(2):
            _, right, left, _ = rings[1 - half]
            third[half, side].wait_recv()
            part = total.at[half, 1 + side, pl.ds(16 * side, 16)]
            part[...] = (
                part[...].astype(jnp.float32) + early_two[half, side].astype(jnp.float32)
            ).astype(jnp.bfloat16)
            fourth[half, side] = go(
                push(
                    total.at[half, 1 + side],
                    late_two.at[half, side],
                    sems[4],
                    half * 2 + side,
                    axes[1 - half],
                    (right, left)[side],
                )
            )
    for half in range(2):
        at = small_at(half, 3)
        for side in range(2):
            fourth[half, side].wait_recv()
        finish(
            half,
            held[half, 3, at].astype(jnp.float32)
            + late[half, 0, at].astype(jnp.float32)
            + late[half, 1, at].astype(jnp.float32)
            + late_two[half, 0].astype(jnp.float32)
            + late_two[half, 1].astype(jnp.float32),
        )
    for copy in copies:
        copy.wait_send()


def scatter_scratch(width):
    return [
        pltpu.VMEM((2, 4, 4, HALF, width), jnp.bfloat16),
        pltpu.VMEM((2, 4, 4, HALF, width), jnp.bfloat16),
        pltpu.VMEM((2, 4, 4, HALF, width), jnp.bfloat16),
        pltpu.VMEM((2, 2, 2, HALF, width), jnp.bfloat16),
        pltpu.VMEM((2, 2, 4, HALF, width), jnp.bfloat16),
        pltpu.VMEM((2, 2, 16, width), jnp.bfloat16),
        pltpu.VMEM((2, 2, HALF, width), jnp.bfloat16),
        pltpu.VMEM((2, 3, HALF, width), jnp.bfloat16),
    ] + [pltpu.SemaphoreType.DMA((n,)) for n in (8, 8, 4, 4, 4, 4, 4, 4, 4, 4)]


def scatter_scope(left_ref, right_ref, scratch, finish, hook=lambda at: None):
    width = right_ref.shape[1]
    depth = right_ref.shape[0]
    tile = 512
    other, held, near, early, late, early_two, late_two, total = scratch[:8]
    flat = scratch[8:]
    sems = [(flat[2 * i], flat[2 * i + 1]) for i in range(5)]

    def make(dst, add, half, core, big):
        if half == 0:
            rows = left_ref[core, big, :, 0:HALF, :]
        else:
            rows = left_ref[core, :, big, HALF:ROWS, :]
        rows = rows.reshape(4 * HALF, depth)

        def column(i, carry):
            cols = pl.ds(pl.multiple_of(i * tile, tile), tile)
            value = jnp.dot(rows, right_ref[:, cols], preferred_element_type=jnp.float32)
            value = value.reshape(4, HALF, tile)
            if add is not None:
                value = value + add[:, :, cols].astype(jnp.float32)
            dst[:, :, cols] = value.astype(jnp.bfloat16)
            return carry

        lax.fori_loop(0, width // tile, column, 0)

    scatter_steps(
        make, other, held, near, early, late, early_two, late_two, total, sems, finish, hook
    )


def mix_kernel(
    left_ref, right_ref, base_ref, gain_ref, part_ref, res_ref, normed_ref, full_ref, *scratch
):
    meet(True)
    spread = Spread(part_ref, full_ref, paired(scratch[18:]))
    spread.send()

    def hook(at):
        if at == 0:
            spread.along()
        else:
            spread.relay()

    def finish(half, value):
        rows = pl.ds(half * HALF, HALF)
        value = value + base_ref[rows, :].astype(jnp.float32)
        res_ref[rows, :] = value
        scaling = lax.rsqrt(jnp.mean(value * value, axis=-1, keepdims=True) + EPSILON)
        normed_ref[rows, :] = (value * scaling * gain_ref[...]).astype(jnp.bfloat16)

    scatter_scope(left_ref, right_ref, scratch[:18], finish, hook)
    spread.arrive()
    spread.done()


def down_kernel(left_ref, right_ref, base_ref, out_ref, *scratch):
    meet()

    def finish(half, value):
        rows = pl.ds(half * HALF, HALF)
        out_ref[rows, :] = (value + base_ref[rows, :]).astype(jnp.bfloat16)

    scatter_scope(left_ref, right_ref, scratch, finish)


VM = pl.BlockSpec(memory_space=pltpu.VMEM)


def remote_params(number):
    return pltpu.CompilerParams(
        collective_id=number, has_side_effects=True, vmem_limit_bytes=60 * 1024 * 1024
    )


def mix(left, right, base, gain, parts):
    width = right.shape[1]
    return pl.pallas_call(
        mix_kernel,
        in_specs=[VM] * 5,
        out_specs=[VM] * 3,
        out_shape=[
            jax.ShapeDtypeStruct((ROWS, width), jnp.float32),
            jax.ShapeDtypeStruct((ROWS, width), jnp.bfloat16),
            jax.ShapeDtypeStruct((16, 4) + parts.shape[1:], jnp.bfloat16),
        ],
        scratch_shapes=scatter_scratch(width) + spread_sems(),
        compiler_params=remote_params(1),
        name="mix",
    )(left.reshape(2, 4, 4, ROWS, -1), right, base, gain.reshape(1, width), parts)


def down(left, right, base):
    width = right.shape[1]
    return pl.pallas_call(
        down_kernel,
        in_specs=[VM] * 3,
        out_specs=VM,
        out_shape=jax.ShapeDtypeStruct((ROWS, width), jnp.bfloat16),
        scratch_shapes=scatter_scratch(width),
        compiler_params=remote_params(2),
        name="down",
    )(left.reshape(2, 4, 4, ROWS, -1), right, base)


def gather_steps(x_ref, buf, sems, use, hook, eager):
    core = lax.axis_index("core")
    axes = ("z", "x")
    rings = (ring("z"), ring("x"))
    copies = []

    def go(copy):
        copy.start()
        copies.append(copy)
        return copy

    def spot(half, big, small, c=None):
        return buf.at[half, big, core if c is None else c, small]

    one = {}
    cores = {}
    for half in range(2):
        big = rings[half][0]
        me, right, left, _ = rings[1 - half]
        buf[half, big, core, me] = x_ref[half * HALF : (half + 1) * HALF, :]
        for side, peer in ((0, right), (1, left)):
            one[half, side] = go(
                push(
                    x_ref.at[pl.ds(half * HALF, HALF)],
                    spot(half, big, me),
                    sems[0],
                    half * 2 + side,
                    axes[1 - half],
                    peer,
                )
            )
        cores[half, 0] = go(
            push(
                x_ref.at[pl.ds(half * HALF, HALF)],
                spot(half, big, me),
                sems[1],
                half * 4,
                "core",
                1 - core,
            )
        )
    hook(0)
    two = {}
    for half in range(2):
        big = rings[half][0]
        me, right, left, far = rings[1 - half]
        for side, (frm, to) in ((0, (left, right)), (1, (right, left))):
            one[half, side].wait_recv()
            piece = buf.at[half, big, core, frm, pl.ds(16 * side, 16)]
            two[half, side] = go(
                push(piece, piece, sems[2], half * 2 + side, axes[1 - half], to)
            )
            whole = spot(half, big, frm)
            cores[half, 1 + side] = go(
                push(whole, whole, sems[1], half * 4 + 1 + side, "core", 1 - core)
            )
    hook(1)
    three = {}
    for half in range(2):
        big, right, left, _ = rings[half]
        far = rings[1 - half][3]
        for side in range(2):
            two[half, side].wait_recv()
        whole = spot(half, big, far)
        chunk = buf.at[half, big, core]
        for side, peer in ((0, right), (1, left)):
            three[half, side] = go(
                push(chunk, chunk, sems[3], half * 2 + side, axes[half], peer)
            )
        cores[half, 3] = go(push(whole, whole, sems[1], half * 4 + 3, "core", 1 - core))
    hook(2)

    def use_own():
        for half in range(2):
            for i in range(4):
                cores[half, i].wait_recv()
            use(half, rings[half][0])

    if not eager:
        use_own()
    four = {}
    fives = {}
    for half in range(2):
        big, right, left, far = rings[half]
        for side, (frm, to) in ((0, (left, right)), (1, (right, left))):
            three[half, side].wait_recv()
            piece = buf.at[half, frm, core, pl.ds(2 * side, 2)]
            four[half, side] = go(push(piece, piece, sems[4], half * 2 + side, axes[half], to))
            chunk = buf.at[half, frm, core]
            fives[half, side] = go(
                push(chunk, chunk, sems[5], half * 4 + side, "core", 1 - core)
            )
    if eager:
        hook(3)
        use_own()
    for half in range(2):
        _, right, left, _ = rings[half]
        for side, frm in ((0, left), (1, right)):
            fives[half, side].wait_recv()
            use(half, frm)
    for half in range(2):
        far = rings[half][3]
        for side in range(2):
            four[half, side].wait_recv()
            piece = buf.at[half, far, core, pl.ds(2 * side, 2)]
            fives[half, 2 + side] = go(
                push(piece, piece, sems[5], half * 4 + 2 + side, "core", 1 - core)
            )
    for half in range(2):
        for side in range(2):
            fives[half, 2 + side].wait_recv()
        use(half, rings[half][3])
    for copy in copies:
        copy.wait_send()


def gather_scratch(width):
    return [pltpu.VMEM((2, 4, 2, 4, HALF, width), jnp.bfloat16)] + [
        pltpu.SemaphoreType.DMA((n,)) for n in (4, 4, 8, 8, 4, 4, 4, 4, 4, 4, 8, 8)
    ]


def gather_scope(x_ref, scratch, use, hook=lambda at: None, eager=False):
    buf = scratch[0]
    sems = [(scratch[1 + 2 * i], scratch[2 + 2 * i]) for i in range(6)]
    gather_steps(x_ref, buf, sems, use, hook, eager)


def project_kernel(x_ref, part_ref, cos_ref, sin_ref, q_ref, kv_ref, full_ref, *scratch):
    meet(True)
    buf = scratch[0]
    spread = Spread(part_ref, full_ref, paired(scratch[13:19]))
    sems = paired(scratch[19:23])
    y, right, left, far = ring_y()
    width = x_ref.shape[1]
    started, passed, copies = [], [], []

    def hook(at):
        if at == 0:
            spread.send()
        elif at == 1:
            spread.along()
        elif at == 2:
            spread.relay()
        else:
            spread.arrive()

    def window(half, big):
        if half == 0:
            return (slice(None), big, slice(None), pl.ds(0, HALF), slice(None))
        return (slice(None), slice(None), big, pl.ds(HALF, HALF), slice(None))

    def flip(value):
        return jnp.concatenate([value[:, HD // 2 :], value[:, : HD // 2]], axis=1)

    def forward(limit):
        while len(passed) < limit:
            index = len(passed)
            half, big, pushes = started[index]
            now = []
            for side, (frm, to) in ((0, (left, right)), (1, (right, left))):
                pushes[side].wait_recv()
                piece = kv_ref.at[(frm, side) + window(half, big)]
                copy = push(piece, piece, sems[1], index * 2 + side, None, at_y(to))
                copy.start()
                copies.append(copy)
                now.append(copy)
            passed.append(now)

    def use(half, big):
        rows = buf[half, big].reshape(8 * HALF, width)
        value = jnp.dot(
            rows, full_ref[...].reshape(width, 3 * 128), preferred_element_type=jnp.float32
        )
        at = window(half, big)
        cosine = cos_ref[at].reshape(8 * HALF, HD)
        sine = sin_ref[at].reshape(8 * HALF, HD)
        shape = (2, 4, HALF, HD)
        query = value[:, 0:HD]
        key = value[:, 128 : 128 + HD]
        q_ref[at] = (query * cosine + flip(query) * sine).astype(jnp.bfloat16).reshape(shape)
        kv_ref[(y, 0) + at] = (
            (key * cosine + flip(key) * sine).astype(jnp.bfloat16).reshape(shape)
        )
        kv_ref[(y, 1) + at] = value[:, 256 : 256 + HD].astype(jnp.bfloat16).reshape(shape)
        index = len(started)
        pushes = []
        for side, peer in ((0, right), (1, left)):
            piece = kv_ref.at[(y, slice(None)) + at]
            copy = push(piece, piece, sems[0], index * 2 + side, None, at_y(peer))
            copy.start()
            copies.append(copy)
            pushes.append(copy)
        started.append((half, big, pushes))
        forward(index)

    gather_scope(x_ref, scratch[:13], use, hook, True)
    forward(8)
    for now in passed:
        for copy in now:
            copy.wait_recv()
    for copy in copies:
        copy.wait_send()
    spread.done()


def lift_kernel(x_ref, w_ref, out_ref, *scratch):
    meet()
    buf = scratch[0]
    units = out_ref.shape[-1]

    def use(half, big):
        rows = buf[half, big].reshape(8 * HALF, x_ref.shape[1])
        value = jnp.dot(rows, w_ref[...], preferred_element_type=jnp.float32)
        gate, up = value[:, :units], value[:, units:]
        value = (gate / (1.0 + jnp.exp(-gate)) * up).astype(jnp.bfloat16)
        value = value.reshape(2, 4, HALF, units)
        if half == 0:
            out_ref[:, big, :, 0:HALF, :] = value
        else:
            out_ref[:, :, big, HALF:ROWS, :] = value

    gather_scope(x_ref, scratch, use)


def project(x, parts, cosine, sine):
    shape = (2, 4, 4, ROWS, HD)
    return pl.pallas_call(
        project_kernel,
        in_specs=[VM] * 4,
        out_specs=[VM] * 2,
        out_shape=[
            jax.ShapeDtypeStruct(shape, jnp.bfloat16),
            jax.ShapeDtypeStruct((4, 2) + shape, jnp.bfloat16),
        ],
        scratch_shapes=[pltpu.VMEM((16, 4) + parts.shape[1:], jnp.bfloat16)]
        + gather_scratch(x.shape[1])
        + spread_sems()
        + [pltpu.SemaphoreType.DMA((16,)) for _ in range(4)],
        compiler_params=remote_params(3),
        name="project",
    )(x, parts, cosine.reshape(shape), sine.reshape(shape))


def lift(x, w):
    units = w.shape[1] // 2
    return pl.pallas_call(
        lift_kernel,
        in_specs=[VM] * 2,
        out_specs=VM,
        out_shape=jax.ShapeDtypeStruct((2, 4, 4, ROWS, units), jnp.bfloat16),
        scratch_shapes=gather_scratch(x.shape[1]),
        compiler_params=remote_params(4),
        name="lift",
    )(x, w).reshape(32 * ROWS, units)


def rope_constants():
    inverse = 1.0 / ROPE_BASE ** (np.arange(0, HD, 2) / HD)

    def table(positions):
        angles = np.asarray(positions, np.float64)[:, None] * inverse[None, :]
        cosine, sine = np.cos(angles), np.sin(angles)
        return np.stack(
            [np.concatenate([cosine, cosine], 1), np.concatenate([-sine, sine], 1)]
        ).astype(np.float32)

    blocks = np.arange(16)
    base = table(np.where(blocks < 16 - SHORT_BLOCKS, blocks * BLOCK, 0))
    at = np.arange(256)
    at = (at // ROWS) * (2 * ROWS) + at % ROWS
    inner = np.stack(
        [
            np.stack([table(at + h * ROWS), table((at + h * ROWS) % SHORT_LEN)])
            for h in range(2)
        ]
    )
    return base[:, :, None, :], inner


PREP = 4


def prep_kernel(
    own_map,
    place,
    x_ref,
    gain_ref,
    *refs,
):
    wide = refs[:5]
    out_ref, down_ref, base_ref, inner_ref = refs[5:9]
    normed_ref, qkv_ref, gu_ref, wout_ref, wdown_ref, cos_ref, sin_ref = refs[9:]
    step = pl.program_id(0)
    core = place[1]
    normed_ref[...] = rms_norm(x_ref[...], gain_ref[...])
    wout_ref[...] = out_ref[...].astype(jnp.bfloat16)
    wdown_ref[...] = down_ref[...].astype(jnp.bfloat16)
    units = gu_ref.shape[2] // 2
    blank = jnp.zeros((qkv_ref.shape[1], 128 - HD), jnp.float32)
    for j in range(4):
        for k in range(2):
            cols = pl.ds(pl.multiple_of((2 * j + core) * units, 128), units)
            gu_ref[j, :, k * units : (k + 1) * units] = wide[3 + k][:, cols].astype(
                jnp.bfloat16
            )
        for k in range(3):
            even = wide[k][:, 2 * j * HD : (2 * j + 1) * HD]
            odd = wide[k][:, (2 * j + 1) * HD : (2 * j + 2) * HD]
            value = jnp.concatenate([jnp.where(core == 0, even, odd), blank], axis=1)
            qkv_ref[j, :, k * 128 : (k + 1) * 128] = value.astype(jnp.bfloat16)
    for j in range(2):
        logical = own_map[2 * step + j]
        kind = (logical >= base_ref.shape[1] - SHORT_BLOCKS).astype(jnp.int32)
        cos_at, sin_at = base_ref[0, logical], base_ref[1, logical]
        cos_in, sin_in = inner_ref[0, kind, 0], inner_ref[0, kind, 1]
        rows = pl.ds(j * 256, 256)
        cos_ref[rows, :] = cos_at * cos_in - sin_at * sin_in
        sin_ref[rows, :] = sin_at * cos_in + cos_at * sin_in


def prep(states, gain, attention_in, attention_out, gate_up, down_weight, own_map, place):
    width = states.shape[1]
    units = down_weight.shape[0]
    quarter = HD // 2
    base, inner = rope_constants()

    def wide(columns, section):
        return pl.BlockSpec(
            (quarter, columns), lambda i, own, at: (at[0], section * PREP + i)
        )

    def across(shape):
        return pl.BlockSpec(shape, lambda i, *_: (0, i))

    def along(shape):
        return pl.BlockSpec(shape, lambda i, *_: (i,) + (0,) * (len(shape) - 1))

    def whole(array):
        return pl.BlockSpec(array.shape, lambda i, *_: (0,) * array.ndim)

    gain = gain.reshape(1, width)
    rows = 32 * ROWS
    return pl.pallas_call(
        prep_kernel,
        grid_spec=pltpu.PrefetchScalarGridSpec(
            num_scalar_prefetch=2,
            grid=(PREP,),
            in_specs=[along((ROWS // PREP, width)), whole(gain)]
            + [wide(8 * HD, k) for k in range(3)]
            + [wide(8 * units, k) for k in range(2)]
            + [
                across((HD, width // PREP)),
                along((units // PREP, width)),
                whole(base),
                pl.BlockSpec(
                    (1,) + inner.shape[1:], lambda i, own, at: (at[2], 0, 0, 0, 0)
                ),
            ],
            out_specs=[
                along((ROWS // PREP, width)),
                along((16 // PREP, quarter, 3 * 128)),
                along((16 // PREP, quarter, 2 * units)),
                across((HD, width // PREP)),
                along((units // PREP, width)),
                along((rows // PREP, HD)),
                along((rows // PREP, HD)),
            ],
        ),
        out_shape=[
            jax.ShapeDtypeStruct((ROWS, width), jnp.bfloat16),
            jax.ShapeDtypeStruct((16, quarter, 3 * 128), jnp.bfloat16),
            jax.ShapeDtypeStruct((16, quarter, 2 * units), jnp.bfloat16),
            jax.ShapeDtypeStruct((HD, width), jnp.bfloat16),
            jax.ShapeDtypeStruct((units, width), jnp.bfloat16),
            jax.ShapeDtypeStruct((rows, HD), jnp.float32),
            jax.ShapeDtypeStruct((rows, HD), jnp.float32),
        ],
        compiler_params=pltpu.CompilerParams(vmem_limit_bytes=48 * 1024 * 1024),
        name="prep",
    )(
        own_map,
        place,
        states,
        gain,
        attention_in,
        attention_in,
        attention_in,
        gate_up,
        gate_up,
        attention_out,
        down_weight,
        base,
        inner,
    )


def body(
    states,
    attention_gain,
    forward_gain,
    attention_in,
    attention_out,
    gate_up,
    down_weight,
    block_map,
    prompt_lengths,
):
    width = states.shape[1]
    units = down_weight.shape[0]
    core = lax.axis_index("core")
    y_hi = lax.axis_index("y_hi")
    y_lo = lax.axis_index("y_lo")
    blocks = block_map.shape[0]
    long_blocks = blocks - SHORT_BLOCKS
    rows = 32 * ROWS

    swap = [
        (((a * 2 + c) * 2 + b), (((1 - a) * 2 + (1 - c)) * 2 + (1 - b)))
        for a in range(2)
        for c in range(2)
        for b in range(2)
        if b != c
    ]

    own_map = lax.dynamic_slice_in_dim(block_map, y_lo * 8, 8)
    normed, qkv_parts, gu_parts, w_out, w_down, cosine, sine = prep(
        states,
        attention_gain,
        attention_in,
        attention_out,
        gate_up,
        down_weight,
        own_map,
        jnp.stack([y_lo, core, y_hi]).astype(jnp.int32),
    )

    def own(narrow):
        other = lax.ppermute(narrow, ("y_lo", "core", "y_hi"), swap)
        return jnp.where(y_hi == core, narrow, other)

    w_out = own(w_out)
    w_down = own(w_down)

    at = jnp.arange(256, dtype=jnp.int32)
    at = (at // ROWS) * (2 * ROWS) + at % ROWS
    q, kv_all = project(normed, qkv_parts, cosine, sine)

    offsets = jnp.concatenate([at, at + ROWS])
    prompt = (own_map - long_blocks)[:, None] * (BLOCK // SHORT_LEN) + offsets[None] // SHORT_LEN
    matches = prompt[:, :, None] == jnp.arange(prompt_lengths.shape[0], dtype=jnp.int32)
    length = jnp.sum(jnp.where(matches, prompt_lengths, 0), axis=2)
    live = (offsets[None] % SHORT_LEN < length).astype(jnp.float32)[:, None, :]

    places = jnp.stack([y_hi, y_lo]).astype(jnp.int32)
    attended = attention(
        q.reshape(8, 256, HD),
        kv_all.reshape(4, 2, 8, 256, HD),
        own_map,
        inverse_map(block_map),
        places,
        live,
    ).reshape(rows, HD)

    group = lax.dynamic_index_in_dim(
        kv_all.reshape(2, 2, 2, 2, 4, 4, ROWS, HD), y_lo, 1, False
    )

    def cache_rows(target):
        picked = lax.dynamic_index_in_dim(group, target, 2, False)
        return jnp.transpose(picked, (1, 2, 3, 0, 4, 5)).reshape(2, rows, HD)

    partner = lax.ppermute(
        cache_rows(1 - core),
        ("core", "y_hi"),
        [(b * 2 + b, (1 - b) * 2 + b) for b in range(2)],
    )
    cache = jnp.where(core == y_hi, cache_rows(core), partner)

    residual, normed_two, w_gu = mix(attended, w_out, states, forward_gain, gu_parts)
    activated = lift(normed_two, w_gu.reshape(width, 2 * units))
    hidden_out = down(activated, w_down, residual)
    return (hidden_out, cache[0], cache[1])


def solution(mesh):
    fine = Mesh(mesh.devices.reshape(2, 2, 4, 4, 2), ("y_lo", "core", "z", "x", "y_hi"))
    hid = ("z", "x", "y_hi")
    grp = ("y_lo", "core")
    in_specs = (
        P(grp + hid, None),
        P(),
        P(),
        P(hid, None),
        P(hid, None),
        P(hid, None),
        P(hid, None),
        P(),
        P(),
    )
    out_specs = (P(grp + hid, None), P(grp, hid), P(grp, hid))
    return jax.shard_map(
        body, mesh=fine, in_specs=in_specs, out_specs=out_specs, check_vma=False
    )
```

```python
import functools

import jax
import jax.numpy as jnp
import numpy as np
from jax import lax
from jax.experimental import pallas as pl
from jax.experimental.pallas import tpu as pltpu
from jax.sharding import Mesh, PartitionSpec as P

HD = 96
BLOCK = 512
SHORT_LEN = 32
WINDOW = 4096
SINKS = 4
SHORT_BLOCKS = 2
EPSILON = 1e-05
ROPE_BASE = 10000.0
MASK_FLOOR = -1e30
LOG2E = 1.4426950408889634

ROWS = 64
PLANE = ("core", "z", "x")


def rms_norm(values, gain):
    widened = values.astype(jnp.float32)
    scaling = lax.rsqrt(jnp.mean(widened * widened, axis=-1, keepdims=True) + EPSILON)
    return (widened * scaling * gain).astype(jnp.bfloat16)


def inverse_map(block_map):
    numbers = jnp.arange(block_map.shape[0], dtype=jnp.int32)
    matches = block_map[None, :] == numbers[:, None]
    return jnp.sum(jnp.where(matches, numbers[None, :], 0), axis=1)


def attention_kernel(
    own_map, slot_of, half_ref, q_ref, kv_ref, live_ref, o_ref, m_ref, l_ref, acc_ref
):
    step = pl.program_id(0)
    logical = own_map[step]
    own_half = half_ref[0]
    own_lo = half_ref[1]
    scale = HD ** (-0.5) * LOG2E
    rows = q_ref.shape[1]
    q = q_ref[0]

    row_at = lax.broadcasted_iota(jnp.int32, (rows, 2 * rows), 0)
    col_at = lax.broadcasted_iota(jnp.int32, (rows, 2 * rows), 1)
    row_off = (row_at // ROWS) * (2 * ROWS) + own_half * ROWS + row_at % ROWS
    col_in = col_at % rows
    col_off = (col_in // ROWS) * (2 * ROWS) + (col_at // rows) * ROWS + col_in % ROWS

    def pair(slot):
        low = slot // 8
        inner = slot % 8
        keys = jnp.concatenate([kv_ref[low, 0, inner], kv_ref[low + 2, 0, inner]], axis=0)
        values = jnp.concatenate([kv_ref[low, 1, inner], kv_ref[low + 2, 1, inner]], axis=0)
        return keys, values

    def scores_of(keys):
        return (
            lax.dot_general(
                q, keys, (((1,), (1,)), ((), ())), preferred_element_type=jnp.float32
            )
            * scale
        )

    def first(scores, values):
        peak = jnp.max(scores, axis=1, keepdims=True)
        weights = jnp.exp2(scores - peak)
        m_ref[...] = peak
        l_ref[...] = jnp.sum(weights, axis=1, keepdims=True)
        acc_ref[...] = jnp.dot(
            weights.astype(jnp.bfloat16), values, preferred_element_type=jnp.float32
        )

    def more(scores, values):
        old = m_ref[...]
        peak = jnp.maximum(old, jnp.max(scores, axis=1, keepdims=True))
        fade = jnp.exp2(old - peak)
        weights = jnp.exp2(scores - peak)
        m_ref[...] = peak
        l_ref[...] = l_ref[...] * fade + jnp.sum(weights, axis=1, keepdims=True)
        acc_ref[...] = acc_ref[...] * fade + jnp.dot(
            weights.astype(jnp.bfloat16), values, preferred_element_type=jnp.float32
        )

    is_long = logical < slot_of.shape[0] - SHORT_BLOCKS
    own_slot = own_lo * 8 + step

    @pl.when(jnp.logical_not(is_long))
    def _():
        keys, values = pair(own_slot)
        allowed = (row_off // SHORT_LEN == col_off // SHORT_LEN) & (col_off <= row_off)
        allowed = allowed & (live_ref[0] > 0.0)
        first(jnp.where(allowed, scores_of(keys), MASK_FLOOR), values)

    @pl.when(is_long)
    def _():
        keys, values = pair(own_slot)
        first(jnp.where(col_off <= row_off, scores_of(keys), MASK_FLOOR), values)
        span = WINDOW // BLOCK
        oldest = jnp.maximum(logical - span + 1, 0)

        def whole(index, carry):
            keys, values = pair(slot_of[index])
            more(scores_of(keys), values)
            return carry

        lax.fori_loop(oldest, logical, whole, 0)

        @pl.when(logical >= span)
        def _():
            edge = logical - span
            keys, values = pair(slot_of[edge])
            allowed = (col_off > row_off) | (edge * BLOCK + col_off < SINKS)
            more(jnp.where(allowed, scores_of(keys), MASK_FLOOR), values)

        @pl.when(logical > span)
        def _():
            slot = slot_of[0]
            keys = kv_ref[slot // 8, 0, slot % 8, 0:128]
            values = kv_ref[slot // 8, 1, slot % 8, 0:128]
            allowed = lax.broadcasted_iota(jnp.int32, (rows, 128), 1) < SINKS
            more(jnp.where(allowed, scores_of(keys), MASK_FLOOR), values)

    o_ref[0] = (acc_ref[...] / l_ref[...]).astype(jnp.bfloat16)


def attention(q, kv, own_map, slot_of, places, live):
    slots, rows, _ = q.shape
    return pl.pallas_call(
        attention_kernel,
        grid_spec=pltpu.PrefetchScalarGridSpec(
            num_scalar_prefetch=3,
            grid=(slots,),
            in_specs=[
                pl.BlockSpec((1, rows, HD), lambda i, *_: (i, 0, 0)),
                pl.BlockSpec(kv.shape, lambda i, *_: (0, 0, 0, 0, 0)),
                pl.BlockSpec((1, 1, 2 * rows), lambda i, *_: (i, 0, 0)),
            ],
            out_specs=pl.BlockSpec((1, rows, HD), lambda i, *_: (i, 0, 0)),
            scratch_shapes=[
                pltpu.VMEM((rows, 1), jnp.float32),
                pltpu.VMEM((rows, 1), jnp.float32),
                pltpu.VMEM((rows, HD), jnp.float32),
            ],
        ),
        out_shape=jax.ShapeDtypeStruct(q.shape, jnp.bfloat16),
        cost_estimate=pl.CostEstimate(
            flops=8_000_000_000, bytes_accessed=8_000_000, transcendentals=8_000_000
        ),
        name="attention",
    )(own_map, slot_of, places, q, kv, live)


MESH = pl.DeviceIdType.MESH
HALF = ROWS // 2


def ring(axis):
    me = lax.axis_index(axis)
    return me, lax.rem(me + 1, 4), lax.rem(me + 3, 4), lax.rem(me + 2, 4)


def ring_y():
    me = lax.axis_index("y_hi") * 2 + lax.axis_index("y_lo")
    return me, lax.rem(me + 1, 4), lax.rem(me + 3, 4), lax.rem(me + 2, 4)


def at_y(y):
    return {"y_hi": lax.div(y, 2), "y_lo": lax.rem(y, 2)}


def at_offset(offset):
    z, x = lax.axis_index("z"), lax.axis_index("x")
    return {"z": lax.rem(z + offset // 4, 4), "x": lax.rem(x + offset % 4, 4)}


def meet(whole=False):
    barrier = pltpu.get_barrier_semaphore()
    peers = [{"core": 1 - lax.axis_index("core")}]
    if whole:
        peers += [at_offset(offset) for offset in range(1, 16)]
        peers += [at_y(y) for y in ring_y()[1:3]]
    else:
        for axis in ("x", "z"):
            peers += [{axis: peer} for peer in ring(axis)[1:3]]
    for peer in peers:
        pl.semaphore_signal(barrier, inc=1, device_id=peer, device_id_type=MESH)
    pl.semaphore_wait(barrier, len(peers))


def push(src, dst, sems, at, axis, peer):
    send, recv = sems
    place = peer if axis is None else {axis: peer}
    return pltpu.make_async_remote_copy(
        src_ref=src,
        dst_ref=dst,
        send_sem=send.at[at],
        recv_sem=recv.at[at],
        device_id=place,
        device_id_type=MESH,
    )


class Spread:
    def __init__(self, parts, full, sems):
        self.parts, self.full, self.sems = parts, full, sems
        self.copies = []

    def go(self, copy):
        copy.start()
        self.copies.append(copy)
        return copy

    def send(self):
        me = lax.axis_index("z") * 4 + lax.axis_index("x")
        y = ring_y()[0]
        self.full[me, y] = self.parts[me]
        self.one = []
        for offset in range(1, 16):
            place = at_offset(offset)
            self.one.append(
                self.go(
                    push(
                        self.parts.at[place["z"] * 4 + place["x"]],
                        self.full.at[me, y],
                        self.sems[0],
                        offset,
                        None,
                        place,
                    )
                )
            )

    def along(self):
        for copy in self.one:
            copy.wait_recv()
        me, right, left, _ = ring_y()
        piece = self.full.at[:, me]
        self.two = [
            self.go(push(piece, piece, self.sems[1], side, None, at_y(peer)))
            for side, peer in ((0, right), (1, left))
        ]

    def relay(self):
        _, right, left, _ = ring_y()
        self.three = []
        for side, (frm, to) in ((0, (left, right)), (1, (right, left))):
            self.two[side].wait_recv()
            piece = self.full.at[pl.ds(8 * side, 8), frm]
            self.three.append(
                self.go(push(piece, piece, self.sems[2], side, None, at_y(to)))
            )

    def arrive(self):
        for copy in self.three:
            copy.wait_recv()

    def done(self):
        for copy in self.copies:
            copy.wait_send()


def spread_sems():
    return [pltpu.SemaphoreType.DMA((n,)) for n in (16, 16, 2, 2, 2, 2)]


def paired(flat):
    return [(flat[2 * i], flat[2 * i + 1]) for i in range(len(flat) // 2)]


def scatter_steps(
    make, other, held, near, early, late, early_two, late_two, total, sems, finish, hook
):
    core = lax.axis_index("core")
    rings = (ring("z"), ring("x"))
    axes = ("z", "x")
    copies = []

    def go(copy):
        copy.start()
        copies.append(copy)
        return copy

    def big_at(half, step):
        me, right, left, far = rings[half]
        return (far, right, left, me)[step]

    swaps = {}

    def hand_over(step):
        for half in range(2):
            at = half * 4 + step
            make(other.at[half, step], None, half, 1 - core, big_at(half, step))
            swaps[half, step] = go(
                push(
                    other.at[half, step],
                    near.at[half, step],
                    sems[0],
                    at,
                    "core",
                    1 - core,
                )
            )

    hand_over(0)
    hand_over(1)
    first = {}
    second = {}
    for half in range(2):
        _, right, left, _ = rings[half]
        swaps[half, 0].wait_recv()
        make(held.at[half, 0], near.at[half, 0], half, core, big_at(half, 0))
        for side, peer in ((0, right), (1, left)):
            first[half, side] = go(
                push(
                    held.at[half, 0, pl.ds(2 * side, 2)],
                    early.at[half, side],
                    sems[1],
                    half * 2 + side,
                    axes[half],
                    peer,
                )
            )
    hand_over(2)
    hand_over(3)

    def pass_on(half, side, quarter):
        _, right, left, _ = rings[half]
        two = pl.ds(2 * quarter, 2)
        second[half, side, quarter] = go(
            push(
                held.at[half, 1 + side, two],
                late.at[half, side, two],
                sems[2],
                (half * 2 + side) * 2 + quarter,
                axes[half],
                (right, left)[side],
            )
        )

    for side in range(2):
        for half in range(2):
            step = 1 + side
            swaps[half, step].wait_recv()
            make(held.at[half, step], near.at[half, step], half, core, big_at(half, step))
            pass_on(half, side, 1 - side)
    hook(0)
    for side in range(2):
        for half in range(2):
            first[half, side].wait_recv()
            part = held.at[half, 1 + side, pl.ds(2 * side, 2)]
            part[...] = (
                part[...].astype(jnp.float32) + early[half, side].astype(jnp.float32)
            ).astype(jnp.bfloat16)
            pass_on(half, side, side)
    hook(1)
    for half in range(2):
        swaps[half, 3].wait_recv()
        make(held.at[half, 3], near.at[half, 3], half, core, big_at(half, 3))

    def small_at(half, step):
        me, right, left, far = rings[1 - half]
        return (far, right, left, me)[step]

    third = {}
    fourth = {}

    def gather_small(half, step):
        at = small_at(half, step)
        total[half, step] = (
            held[half, 3, at].astype(jnp.float32)
            + late[half, 0, at].astype(jnp.float32)
            + late[half, 1, at].astype(jnp.float32)
        ).astype(jnp.bfloat16)

    for half in range(2):
        _, right, left, _ = rings[1 - half]
        for side in range(2):
            for quarter in range(2):
                second[half, side, quarter].wait_recv()
        gather_small(half, 0)
        for side, peer in ((0, right), (1, left)):
            third[half, side] = go(
                push(
                    total.at[half, 0, pl.ds(16 * side, 16)],
                    early_two.at[half, side],
                    sems[3],
                    half * 2 + side,
                    axes[1 - half],
                    peer,
                )
            )
        gather_small(half, 1)
        gather_small(half, 2)
    for side in range(2):
        for half in range(2):
            _, right, left, _ = rings[1 - half]
            third[half, side].wait_recv()
            part = total.at[half, 1 + side, pl.ds(16 * side, 16)]
            part[...] = (
                part[...].astype(jnp.float32) + early_two[half, side].astype(jnp.float32)
            ).astype(jnp.bfloat16)
            fourth[half, side] = go(
                push(
                    total.at[half, 1 + side],
                    late_two.at[half, side],
                    sems[4],
                    half * 2 + side,
                    axes[1 - half],
                    (right, left)[side],
                )
            )
    for half in range(2):
        at = small_at(half, 3)
        for side in range(2):
            fourth[half, side].wait_recv()
        finish(
            half,
            held[half, 3, at].astype(jnp.float32)
            + late[half, 0, at].astype(jnp.float32)
            + late[half, 1, at].astype(jnp.float32)
            + late_two[half, 0].astype(jnp.float32)
            + late_two[half, 1].astype(jnp.float32),
        )
    for copy in copies:
        copy.wait_send()


def scatter_scratch(width):
    return [
        pltpu.VMEM((2, 4, 4, HALF, width), jnp.bfloat16),
        pltpu.VMEM((2, 4, 4, HALF, width), jnp.bfloat16),
        pltpu.VMEM((2, 4, 4, HALF, width), jnp.bfloat16),
        pltpu.VMEM((2, 2, 2, HALF, width), jnp.bfloat16),
        pltpu.VMEM((2, 2, 4, HALF, width), jnp.bfloat16),
        pltpu.VMEM((2, 2, 16, width), jnp.bfloat16),
        pltpu.VMEM((2, 2, HALF, width), jnp.bfloat16),
        pltpu.VMEM((2, 3, HALF, width), jnp.bfloat16),
    ] + [pltpu.SemaphoreType.DMA((n,)) for n in (8, 8, 4, 4, 8, 8, 4, 4, 4, 4)]


def scatter_scope(left_ref, right_ref, scratch, finish, hook=lambda at: None):
    width = right_ref.shape[1]
    depth = right_ref.shape[0]
    tile = 512
    other, held, near, early, late, early_two, late_two, total = scratch[:8]
    flat = scratch[8:]
    sems = [(flat[2 * i], flat[2 * i + 1]) for i in range(5)]

    def make(dst, add, half, core, big):
        if half == 0:
            rows = left_ref[core, big, :, 0:HALF, :]
        else:
            rows = left_ref[core, :, big, HALF:ROWS, :]
        rows = rows.reshape(4 * HALF, depth)

        def column(i, carry):
            cols = pl.ds(pl.multiple_of(i * tile, tile), tile)
            value = jnp.dot(rows, right_ref[:, cols], preferred_element_type=jnp.float32)
            value = value.reshape(4, HALF, tile)
            if add is not None:
                value = value + add[:, :, cols].astype(jnp.float32)
            dst[:, :, cols] = value.astype(jnp.bfloat16)
            return carry

        lax.fori_loop(0, width // tile, column, 0)

    scatter_steps(
        make, other, held, near, early, late, early_two, late_two, total, sems, finish, hook
    )


def mix_kernel(
    left_ref, right_ref, base_ref, gain_ref, part_ref, res_ref, normed_ref, full_ref, *scratch
):
    meet(True)
    spread = Spread(part_ref, full_ref, paired(scratch[18:]))
    spread.send()

    def hook(at):
        if at == 0:
            spread.along()
        else:
            spread.relay()

    def finish(half, value):
        rows = pl.ds(half * HALF, HALF)
        value = value + base_ref[rows, :].astype(jnp.float32)
        res_ref[rows, :] = value
        scaling = lax.rsqrt(jnp.mean(value * value, axis=-1, keepdims=True) + EPSILON)
        normed_ref[rows, :] = (value * scaling * gain_ref[...]).astype(jnp.bfloat16)

    scatter_scope(left_ref, right_ref, scratch[:18], finish, hook)
    spread.arrive()
    spread.done()


def down_kernel(left_ref, right_ref, base_ref, out_ref, *scratch):
    meet()

    def finish(half, value):
        rows = pl.ds(half * HALF, HALF)
        out_ref[rows, :] = (value + base_ref[rows, :]).astype(jnp.bfloat16)

    scatter_scope(left_ref, right_ref, scratch, finish)


VM = pl.BlockSpec(memory_space=pltpu.VMEM)


def remote_params(number):
    return pltpu.CompilerParams(
        collective_id=number, has_side_effects=True, vmem_limit_bytes=60 * 1024 * 1024
    )


def mix(left, right, base, gain, parts):
    width = right.shape[1]
    return pl.pallas_call(
        mix_kernel,
        in_specs=[VM] * 5,
        out_specs=[VM] * 3,
        out_shape=[
            jax.ShapeDtypeStruct((ROWS, width), jnp.float32),
            jax.ShapeDtypeStruct((ROWS, width), jnp.bfloat16),
            jax.ShapeDtypeStruct((16, 4) + parts.shape[1:], jnp.bfloat16),
        ],
        scratch_shapes=scatter_scratch(width) + spread_sems(),
        compiler_params=remote_params(1),
        name="mix",
    )(left.reshape(2, 4, 4, ROWS, -1), right, base, gain.reshape(1, width), parts)


def down(left, right, base):
    width = right.shape[1]
    return pl.pallas_call(
        down_kernel,
        in_specs=[VM] * 3,
        out_specs=VM,
        out_shape=jax.ShapeDtypeStruct((ROWS, width), jnp.bfloat16),
        scratch_shapes=scatter_scratch(width),
        compiler_params=remote_params(2),
        name="down",
    )(left.reshape(2, 4, 4, ROWS, -1), right, base)


def gather_steps(x_ref, buf, sems, use, hook, eager):
    core = lax.axis_index("core")
    axes = ("z", "x")
    rings = (ring("z"), ring("x"))
    copies = []

    def go(copy):
        copy.start()
        copies.append(copy)
        return copy

    def spot(half, big, small, c=None):
        return buf.at[half, big, core if c is None else c, small]

    one = {}
    cores = {}
    for half in range(2):
        big = rings[half][0]
        me, right, left, _ = rings[1 - half]
        buf[half, big, core, me] = x_ref[half * HALF : (half + 1) * HALF, :]
        for side, peer in ((0, right), (1, left)):
            one[half, side] = go(
                push(
                    x_ref.at[pl.ds(half * HALF, HALF)],
                    spot(half, big, me),
                    sems[0],
                    half * 2 + side,
                    axes[1 - half],
                    peer,
                )
            )
        cores[half, 0] = go(
            push(
                x_ref.at[pl.ds(half * HALF, HALF)],
                spot(half, big, me),
                sems[1],
                half * 4,
                "core",
                1 - core,
            )
        )
    hook(0)
    two = {}
    for half in range(2):
        big = rings[half][0]
        me, right, left, far = rings[1 - half]
        for side, (frm, to) in ((0, (left, right)), (1, (right, left))):
            one[half, side].wait_recv()
            piece = buf.at[half, big, core, frm, pl.ds(16 * side, 16)]
            two[half, side] = go(
                push(piece, piece, sems[2], half * 2 + side, axes[1 - half], to)
            )
            whole = spot(half, big, frm)
            cores[half, 1 + side] = go(
                push(whole, whole, sems[1], half * 4 + 1 + side, "core", 1 - core)
            )
    hook(1)
    three = {}
    for half in range(2):
        big, right, left, _ = rings[half]
        far = rings[1 - half][3]
        for side in range(2):
            two[half, side].wait_recv()
        whole = spot(half, big, far)
        chunk = buf.at[half, big, core]
        for side, peer in ((0, right), (1, left)):
            three[half, side] = go(
                push(chunk, chunk, sems[3], half * 2 + side, axes[half], peer)
            )
        cores[half, 3] = go(push(whole, whole, sems[1], half * 4 + 3, "core", 1 - core))
    hook(2)

    def use_own():
        for half in range(2):
            for i in range(4):
                cores[half, i].wait_recv()
            use(half, rings[half][0])

    if not eager:
        use_own()
    four = {}
    fives = {}
    for half in range(2):
        big, right, left, far = rings[half]
        for side, (frm, to) in ((0, (left, right)), (1, (right, left))):
            three[half, side].wait_recv()
            piece = buf.at[half, frm, core, pl.ds(2 * side, 2)]
            four[half, side] = go(push(piece, piece, sems[4], half * 2 + side, axes[half], to))
            chunk = buf.at[half, frm, core]
            fives[half, side] = go(
                push(chunk, chunk, sems[5], half * 4 + side, "core", 1 - core)
            )
    if eager:
        hook(3)
        use_own()
    for half in range(2):
        _, right, left, _ = rings[half]
        for side, frm in ((0, left), (1, right)):
            fives[half, side].wait_recv()
            use(half, frm)
    for half in range(2):
        far = rings[half][3]
        for side in range(2):
            four[half, side].wait_recv()
            piece = buf.at[half, far, core, pl.ds(2 * side, 2)]
            fives[half, 2 + side] = go(
                push(piece, piece, sems[5], half * 4 + 2 + side, "core", 1 - core)
            )
    for half in range(2):
        for side in range(2):
            fives[half, 2 + side].wait_recv()
        use(half, rings[half][3])
    for copy in copies:
        copy.wait_send()


def gather_scratch(width):
    return [pltpu.VMEM((2, 4, 2, 4, HALF, width), jnp.bfloat16)] + [
        pltpu.SemaphoreType.DMA((n,)) for n in (4, 4, 8, 8, 4, 4, 4, 4, 4, 4, 8, 8)
    ]


def gather_scope(x_ref, scratch, use, hook=lambda at: None, eager=False):
    buf = scratch[0]
    sems = [(scratch[1 + 2 * i], scratch[2 + 2 * i]) for i in range(6)]
    gather_steps(x_ref, buf, sems, use, hook, eager)


def project_kernel(x_ref, part_ref, cos_ref, sin_ref, q_ref, kv_ref, full_ref, *scratch):
    meet(True)
    buf = scratch[0]
    spread = Spread(part_ref, full_ref, paired(scratch[13:19]))
    sems = paired(scratch[19:23])
    y, right, left, far = ring_y()
    width = x_ref.shape[1]
    started, passed, copies = [], [], []

    def hook(at):
        if at == 0:
            spread.send()
        elif at == 1:
            spread.along()
        elif at == 2:
            spread.relay()
        else:
            spread.arrive()

    def window(half, big):
        if half == 0:
            return (slice(None), big, slice(None), pl.ds(0, HALF), slice(None))
        return (slice(None), slice(None), big, pl.ds(HALF, HALF), slice(None))

    def flip(value):
        return jnp.concatenate([value[:, HD // 2 :], value[:, : HD // 2]], axis=1)

    def forward(limit):
        while len(passed) < limit:
            index = len(passed)
            half, big, pushes = started[index]
            now = []
            for side, (frm, to) in ((0, (left, right)), (1, (right, left))):
                pushes[side].wait_recv()
                piece = kv_ref.at[(frm, side) + window(half, big)]
                copy = push(piece, piece, sems[1], index * 2 + side, None, at_y(to))
                copy.start()
                copies.append(copy)
                now.append(copy)
            passed.append(now)

    def use(half, big):
        rows = buf[half, big].reshape(8 * HALF, width)
        value = jnp.dot(
            rows, full_ref[...].reshape(width, 3 * 128), preferred_element_type=jnp.float32
        )
        at = window(half, big)
        cosine = cos_ref[at].reshape(8 * HALF, HD)
        sine = sin_ref[at].reshape(8 * HALF, HD)
        shape = (2, 4, HALF, HD)
        query = value[:, 0:HD]
        key = value[:, 128 : 128 + HD]
        q_ref[at] = (query * cosine + flip(query) * sine).astype(jnp.bfloat16).reshape(shape)
        kv_ref[(y, 0) + at] = (
            (key * cosine + flip(key) * sine).astype(jnp.bfloat16).reshape(shape)
        )
        kv_ref[(y, 1) + at] = value[:, 256 : 256 + HD].astype(jnp.bfloat16).reshape(shape)
        index = len(started)
        pushes = []
        for side, peer in ((0, right), (1, left)):
            piece = kv_ref.at[(y, slice(None)) + at]
            copy = push(piece, piece, sems[0], index * 2 + side, None, at_y(peer))
            copy.start()
            copies.append(copy)
            pushes.append(copy)
        started.append((half, big, pushes))
        forward(index)

    gather_scope(x_ref, scratch[:13], use, hook, True)
    forward(8)
    for now in passed:
        for copy in now:
            copy.wait_recv()
    for copy in copies:
        copy.wait_send()
    spread.done()


def lift_kernel(x_ref, w_ref, out_ref, *scratch):
    meet()
    buf = scratch[0]
    units = out_ref.shape[-1]

    def use(half, big):
        rows = buf[half, big].reshape(8 * HALF, x_ref.shape[1])
        value = jnp.dot(rows, w_ref[...], preferred_element_type=jnp.float32)
        gate, up = value[:, :units], value[:, units:]
        value = (gate / (1.0 + jnp.exp(-gate)) * up).astype(jnp.bfloat16)
        value = value.reshape(2, 4, HALF, units)
        if half == 0:
            out_ref[:, big, :, 0:HALF, :] = value
        else:
            out_ref[:, :, big, HALF:ROWS, :] = value

    gather_scope(x_ref, scratch, use)


def project(x, parts, cosine, sine):
    shape = (2, 4, 4, ROWS, HD)
    return pl.pallas_call(
        project_kernel,
        in_specs=[VM] * 4,
        out_specs=[VM] * 2,
        out_shape=[
            jax.ShapeDtypeStruct(shape, jnp.bfloat16),
            jax.ShapeDtypeStruct((4, 2) + shape, jnp.bfloat16),
        ],
        scratch_shapes=[pltpu.VMEM((16, 4) + parts.shape[1:], jnp.bfloat16)]
        + gather_scratch(x.shape[1])
        + spread_sems()
        + [pltpu.SemaphoreType.DMA((16,)) for _ in range(4)],
        compiler_params=remote_params(3),
        name="project",
    )(x, parts, cosine.reshape(shape), sine.reshape(shape))


def lift(x, w):
    units = w.shape[1] // 2
    return pl.pallas_call(
        lift_kernel,
        in_specs=[VM] * 2,
        out_specs=VM,
        out_shape=jax.ShapeDtypeStruct((2, 4, 4, ROWS, units), jnp.bfloat16),
        scratch_shapes=gather_scratch(x.shape[1]),
        compiler_params=remote_params(4),
        name="lift",
    )(x, w).reshape(32 * ROWS, units)


def rope_constants():
    inverse = 1.0 / ROPE_BASE ** (np.arange(0, HD, 2) / HD)

    def table(positions):
        angles = np.asarray(positions, np.float64)[:, None] * inverse[None, :]
        cosine, sine = np.cos(angles), np.sin(angles)
        return np.stack(
            [np.concatenate([cosine, cosine], 1), np.concatenate([-sine, sine], 1)]
        ).astype(np.float32)

    blocks = np.arange(16)
    base = table(np.where(blocks < 16 - SHORT_BLOCKS, blocks * BLOCK, 0))
    at = np.arange(256)
    at = (at // ROWS) * (2 * ROWS) + at % ROWS
    inner = np.stack(
        [
            np.stack([table(at + h * ROWS), table((at + h * ROWS) % SHORT_LEN)])
            for h in range(2)
        ]
    )
    return base[:, :, None, :], inner


PREP = 4


def prep_kernel(
    own_map,
    place,
    x_ref,
    gain_ref,
    *refs,
):
    wide = refs[:5]
    out_ref, down_ref, base_ref, inner_ref = refs[5:9]
    normed_ref, qkv_ref, gu_ref, wout_ref, wdown_ref, cos_ref, sin_ref = refs[9:]
    step = pl.program_id(0)
    core = place[1]
    normed_ref[...] = rms_norm(x_ref[...], gain_ref[...])
    wout_ref[...] = out_ref[...].astype(jnp.bfloat16)
    wdown_ref[...] = down_ref[...].astype(jnp.bfloat16)
    units = gu_ref.shape[2] // 2
    blank = jnp.zeros((qkv_ref.shape[1], 128 - HD), jnp.float32)
    for j in range(4):
        for k in range(2):
            cols = pl.ds(pl.multiple_of((2 * j + core) * units, 128), units)
            gu_ref[j, :, k * units : (k + 1) * units] = wide[3 + k][:, cols].astype(
                jnp.bfloat16
            )
        for k in range(3):
            even = wide[k][:, 2 * j * HD : (2 * j + 1) * HD]
            odd = wide[k][:, (2 * j + 1) * HD : (2 * j + 2) * HD]
            value = jnp.concatenate([jnp.where(core == 0, even, odd), blank], axis=1)
            qkv_ref[j, :, k * 128 : (k + 1) * 128] = value.astype(jnp.bfloat16)
    for j in range(2):
        logical = own_map[2 * step + j]
        kind = (logical >= base_ref.shape[1] - SHORT_BLOCKS).astype(jnp.int32)
        cos_at, sin_at = base_ref[0, logical], base_ref[1, logical]
        cos_in, sin_in = inner_ref[0, kind, 0], inner_ref[0, kind, 1]
        rows = pl.ds(j * 256, 256)
        cos_ref[rows, :] = cos_at * cos_in - sin_at * sin_in
        sin_ref[rows, :] = sin_at * cos_in + cos_at * sin_in


def prep(states, gain, attention_in, attention_out, gate_up, down_weight, own_map, place):
    width = states.shape[1]
    units = down_weight.shape[0]
    quarter = HD // 2
    base, inner = rope_constants()

    def wide(columns, section):
        return pl.BlockSpec(
            (quarter, columns), lambda i, own, at: (at[0], section * PREP + i)
        )

    def across(shape):
        return pl.BlockSpec(shape, lambda i, *_: (0, i))

    def along(shape):
        return pl.BlockSpec(shape, lambda i, *_: (i,) + (0,) * (len(shape) - 1))

    def whole(array):
        return pl.BlockSpec(array.shape, lambda i, *_: (0,) * array.ndim)

    gain = gain.reshape(1, width)
    rows = 32 * ROWS
    return pl.pallas_call(
        prep_kernel,
        grid_spec=pltpu.PrefetchScalarGridSpec(
            num_scalar_prefetch=2,
            grid=(PREP,),
            in_specs=[along((ROWS // PREP, width)), whole(gain)]
            + [wide(8 * HD, k) for k in range(3)]
            + [wide(8 * units, k) for k in range(2)]
            + [
                across((HD, width // PREP)),
                along((units // PREP, width)),
                whole(base),
                pl.BlockSpec(
                    (1,) + inner.shape[1:], lambda i, own, at: (at[2], 0, 0, 0, 0)
                ),
            ],
            out_specs=[
                along((ROWS // PREP, width)),
                along((16 // PREP, quarter, 3 * 128)),
                along((16 // PREP, quarter, 2 * units)),
                across((HD, width // PREP)),
                along((units // PREP, width)),
                along((rows // PREP, HD)),
                along((rows // PREP, HD)),
            ],
        ),
        out_shape=[
            jax.ShapeDtypeStruct((ROWS, width), jnp.bfloat16),
            jax.ShapeDtypeStruct((16, quarter, 3 * 128), jnp.bfloat16),
            jax.ShapeDtypeStruct((16, quarter, 2 * units), jnp.bfloat16),
            jax.ShapeDtypeStruct((HD, width), jnp.bfloat16),
            jax.ShapeDtypeStruct((units, width), jnp.bfloat16),
            jax.ShapeDtypeStruct((rows, HD), jnp.float32),
            jax.ShapeDtypeStruct((rows, HD), jnp.float32),
        ],
        compiler_params=pltpu.CompilerParams(vmem_limit_bytes=48 * 1024 * 1024),
        name="prep",
    )(
        own_map,
        place,
        states,
        gain,
        attention_in,
        attention_in,
        attention_in,
        gate_up,
        gate_up,
        attention_out,
        down_weight,
        base,
        inner,
    )


def body(
    states,
    attention_gain,
    forward_gain,
    attention_in,
    attention_out,
    gate_up,
    down_weight,
    block_map,
    prompt_lengths,
):
    width = states.shape[1]
    units = down_weight.shape[0]
    core = lax.axis_index("core")
    y_hi = lax.axis_index("y_hi")
    y_lo = lax.axis_index("y_lo")
    blocks = block_map.shape[0]
    long_blocks = blocks - SHORT_BLOCKS
    rows = 32 * ROWS

    swap = [
        (((a * 2 + c) * 2 + b), (((1 - a) * 2 + (1 - c)) * 2 + (1 - b)))
        for a in range(2)
        for c in range(2)
        for b in range(2)
        if b != c
    ]

    own_map = lax.dynamic_slice_in_dim(block_map, y_lo * 8, 8)
    normed, qkv_parts, gu_parts, w_out, w_down, cosine, sine = prep(
        states,
        attention_gain,
        attention_in,
        attention_out,
        gate_up,
        down_weight,
        own_map,
        jnp.stack([y_lo, core, y_hi]).astype(jnp.int32),
    )

    def own(narrow):
        other = lax.ppermute(narrow, ("y_lo", "core", "y_hi"), swap)
        return jnp.where(y_hi == core, narrow, other)

    w_out = own(w_out)
    w_down = own(w_down)

    at = jnp.arange(256, dtype=jnp.int32)
    at = (at // ROWS) * (2 * ROWS) + at % ROWS
    q, kv_all = project(normed, qkv_parts, cosine, sine)

    offsets = jnp.concatenate([at, at + ROWS])
    prompt = (own_map - long_blocks)[:, None] * (BLOCK // SHORT_LEN) + offsets[None] // SHORT_LEN
    matches = prompt[:, :, None] == jnp.arange(prompt_lengths.shape[0], dtype=jnp.int32)
    length = jnp.sum(jnp.where(matches, prompt_lengths, 0), axis=2)
    live = (offsets[None] % SHORT_LEN < length).astype(jnp.float32)[:, None, :]

    places = jnp.stack([y_hi, y_lo]).astype(jnp.int32)
    attended = attention(
        q.reshape(8, 256, HD),
        kv_all.reshape(4, 2, 8, 256, HD),
        own_map,
        inverse_map(block_map),
        places,
        live,
    ).reshape(rows, HD)

    group = lax.dynamic_index_in_dim(
        kv_all.reshape(2, 2, 2, 2, 4, 4, ROWS, HD), y_lo, 1, False
    )

    def cache_rows(target):
        picked = lax.dynamic_index_in_dim(group, target, 2, False)
        return jnp.transpose(picked, (1, 2, 3, 0, 4, 5)).reshape(2, rows, HD)

    partner = lax.ppermute(
        cache_rows(1 - core),
        ("core", "y_hi"),
        [(b * 2 + b, (1 - b) * 2 + b) for b in range(2)],
    )
    cache = jnp.where(core == y_hi, cache_rows(core), partner)

    residual, normed_two, w_gu = mix(attended, w_out, states, forward_gain, gu_parts)
    activated = lift(normed_two, w_gu.reshape(width, 2 * units))
    hidden_out = down(activated, w_down, residual)
    return (hidden_out, cache[0], cache[1])


def solution(mesh):
    fine = Mesh(mesh.devices.reshape(2, 2, 4, 4, 2), ("y_lo", "core", "z", "x", "y_hi"))
    hid = ("z", "x", "y_hi")
    grp = ("y_lo", "core")
    in_specs = (
        P(grp + hid, None),
        P(),
        P(),
        P(hid, None),
        P(hid, None),
        P(hid, None),
        P(hid, None),
        P(),
        P(),
    )
    out_specs = (P(grp + hid, None), P(grp, hid), P(grp, hid))
    return jax.shard_map(
        body, mesh=fine, in_specs=in_specs, out_specs=out_specs, check_vma=False
    )
```
